128 devices in a mesh: nodes: 128 (over x, y, z, core).
Axes of the slice: x: 4, y: 4, z: 4, core: 2. Of those that a mesh axis runs over, the one named last changes fastest.
Arguments:
- features: bfloat16 [2097152, 128], P('nodes'), may hold values from -6 to 6
- nbr_owner: int32 [4096, 32], P('nodes'), may hold values from 0 to 127, all different within a row; in each aligned block of 32 rows (0 to 31, 32 to 63, ...) at most 16 rows name the same one
- nbr_local: int32 [4096, 32], P('nodes'), may hold values from 0 to 16383
- ppr_weight: float32 [4096, 32], P('nodes'), may hold values from 0.01 to 0.1
- labels: int32 [4096], P('nodes'), may hold values from 0 to 171
- w_first: bfloat16 [128, 512], replicated, may hold values from -0.5 to 0.5
- w_second: bfloat16 [512, 512], replicated, may hold values from -0.25 to 0.25
- w_third: bfloat16 [512, 172], replicated, may hold values from -0.25 to 0.25
Outputs:
- loss: float32 [], replicated
- seed_logits: float32 [4096, 172], P('nodes')
- grad_first: float32 [128, 512], replicated
- grad_second: float32 [512, 512], replicated
- grad_third: float32 [512, 172], replicated
The draws below stay inside these ranges and needn't reach their ends.
Inputs may be any that keep to these rules, and one draw needn't show every extreme that they name: `nbr_owner`: each row names 32 different devices; among the rows of one device no device is named by more than 16 rows.
All inputs are finite; a program needn't handle non-finite values.
Results may differ from the reference program's by a relative error of at most 0.01.
The reference program's roundings to bfloat16 on the way count: a program that leaves them out, or rounds other values in their place, can miss the bound.
Values may be sent and summed in bfloat16 or wider, within the bound.
No kernel may reach another device: no remote copies, remote signals or barrier semaphores. Data moves between devices by JAX's collectives and lax.ppermute only.
A program may use at most 64 MiB of HBM per device.

```python
import math
import jax
import jax.numpy as jnp
import numpy as np

F = 128
H = 512
C = 172
K = 32
SEED_DEV = 32
NODE_DEV = 16384
CAP = 16
SEEDS = 4096
NODES = 2097152
N_NODES = 128


def plant(values, key, least, high):
    longest = values.shape.index(max(values.shape))
    spots = []
    for shift in (0, 1):
        where = [jax.random.randint(jax.random.fold_in(key, axis), (), 0, length) for axis, length in enumerate(values.shape)]
        where[longest] = (where[longest] + shift) % values.shape[longest]
        spots.append(tuple(where))
    return values.at[spots[0]].set(least).at[spots[1]].set(high)


def block_levels(key, shape, split, least, high):
    factor_of, own = 1.0, jax.random.fold_in(key, 6)
    for axis_at, parts in split:
        steps = jnp.exp(jax.random.uniform(jax.random.fold_in(own, axis_at), (parts,), jnp.float32, least / len(split), high / len(split)))
        factor_of = factor_of * jnp.repeat(steps, shape[axis_at] // parts).reshape([-1 if axis == axis_at else 1 for axis in range(len(shape))])
    return factor_of


def assign_block(stream_key, own, number, rows, number_of, top, most, slope):
    order = jax.random.permutation(stream_key, number_of)
    heavy_load, common = shares(number_of, rows * top, most, slope, True), shares(number_of, rows * top, most, slope, False)
    places = jnp.arange(number_of)

    def named(tallies, offset_by):
        used = int((tallies > 0).sum())
        fixed = max(1, used // 4)
        shifted = fixed + (places - fixed + offset_by * (used - fixed)) % max(1, number_of - fixed)
        return jnp.zeros((number_of,), jnp.int32).at[order[jnp.where(places < fixed, places, shifted)]].set(jnp.asarray(tallies, jnp.int32))

    tallies = jnp.where(number % 4 == 0, named(heavy_load, number // 4), named(common, number - number // 4 - 1))
    mixed = jax.random.permutation(jax.random.fold_in(own, 3), number_of)
    giver, receiver = mixed[0:number_of // 2 * 2:2], mixed[1:number_of // 2 * 2:2]
    room = jnp.minimum(tallies[giver] - 1, most - tallies[receiver]) // 2
    room = jnp.where((giver == order[0]) | (receiver == order[0]) | (tallies[receiver] == 0), 0, jnp.maximum(room, 0))
    shifted = jax.random.randint(jax.random.fold_in(own, 4), (number_of // 2,), 0, 1 << 20) % (room + 1)
    tallies = tallies.at[giver].add(-shifted).at[receiver].add(shifted)
    members = jnp.searchsorted(jnp.cumsum(tallies), jnp.arange(rows * top), side="right").astype(jnp.int32)
    grid = members.reshape(top, rows).T
    grid = grid[jax.random.permutation(jax.random.fold_in(own, 1), rows)]
    offset_by = jax.random.randint(jax.random.fold_in(own, 2), (rows, 1), 0, top)
    return jnp.take_along_axis(grid, (jnp.arange(top)[None, :] + offset_by) % top, axis=1)


def shares(number_of, total, most, slope, full):
    loads = [(1 << 20) // math.isqrt(rank ** slope) + 1 for rank in range(1, number_of + 1)]
    largest = most if full else min(most, max(-(-total // number_of), total * loads[0] // sum(loads)))
    least = 1 if total - largest >= number_of - 1 else 0
    given, surplus = [largest] + [least] * (number_of - 1), total - largest - least * (number_of - 1)
    while surplus > 0:
        movable = [i for i in range(1, number_of) if given[i] < largest] or [i for i in range(1, number_of) if given[i] < most]
        whole, budget = sum([loads[i] for i in movable]), surplus
        for i in movable:
            addition = min(most - given[i], max(1, budget * loads[i] // whole), surplus)
            given[i] = given[i] + addition
            surplus = surplus - addition
    return np.array(given)


def noise(rng, shape, spread, limit, split=(), kind=jnp.bfloat16):
    level = block_levels(rng, shape, split, -0.22, 0.18) if split else 1.0
    values = jax.random.normal(rng, shape, jnp.float32) * spread * level
    return jnp.minimum(jnp.maximum(values, -limit), limit).astype(kind)


def setup_inputs(seed: int = 0) -> dict:
    seeds = jax.random.split(jax.random.key(seed), 9)
    features = noise(seeds[0], (NODES, F), 1.0, 6.0, ((0, 128),))
    nbr_owner_keys = jax.random.split(jax.random.fold_in(seeds[1], 1), SEEDS // SEED_DEV)
    nbr_owner_turns = jax.random.permutation(jax.random.fold_in(seeds[1], 3), SEEDS // SEED_DEV)
    nbr_owner = jax.vmap(lambda own, number: assign_block(jax.random.fold_in(seeds[1], 2), own, number, SEED_DEV, N_NODES, K, CAP, 2))(nbr_owner_keys, nbr_owner_turns).reshape((SEEDS, K))
    nbr_local = plant(jax.random.randint(seeds[2], (SEEDS, K), 0, NODE_DEV), jax.random.fold_in(seeds[2], 1), 0, NODE_DEV - 1).astype(jnp.int32)
    ppr_weight = jnp.clip(jnp.exp(math.log(0.1) - 2.3025851 * jax.random.uniform(seeds[3], (SEEDS, K), jnp.float32) ** block_levels(seeds[3], (SEEDS, K), ((0, 128),), -0.2, 0.2)), 0.01, 0.1)
    labels = plant(jax.random.randint(seeds[4], (SEEDS,), 0, C), jax.random.fold_in(seeds[4], 1), 0, C - 1).astype(jnp.int32)
    w_first = noise(seeds[5], (F, H), F ** -0.5, 0.5)
    w_second = noise(seeds[6], (H, H), H ** -0.5, 0.25)
    w_third = noise(seeds[7], (H, C), H ** -0.5, 0.25)
    return {"features": features, "nbr_owner": nbr_owner, "nbr_local": nbr_local, "ppr_weight": ppr_weight, "labels": labels, "w_first": w_first, "w_second": w_second, "w_third": w_third}


def reference(features, nbr_owner, nbr_local, ppr_weight, labels, w_first, w_second, w_third):
    node_index = (nbr_owner * NODE_DEV + nbr_local).reshape(-1).astype(jnp.int32)
    row_block = jnp.take(features, node_index, axis=0)
    first_pre = jnp.dot(row_block, w_first, preferred_element_type=jnp.float32)
    first_act = jnp.maximum(first_pre, 0.0).astype(jnp.bfloat16)
    second_pre = jnp.dot(first_act, w_second, preferred_element_type=jnp.float32)
    second_act = jnp.maximum(second_pre, 0.0).astype(jnp.bfloat16)
    row_logits = jnp.dot(second_act, w_third, preferred_element_type=jnp.float32)
    seed_logits = jnp.sum(ppr_weight[:, :, None] * row_logits.reshape(SEEDS, K, C), axis=1)
    highest = jnp.max(seed_logits, axis=1, keepdims=True)
    log_total = jnp.log(jnp.sum(jnp.exp(seed_logits - highest), axis=1, keepdims=True)) + highest
    onehot = (labels[:, None] == jnp.arange(C, dtype=jnp.int32)[None, :]).astype(jnp.float32)
    loss = jnp.sum(log_total[:, 0] - jnp.sum(onehot * seed_logits, axis=1)) / SEEDS
    logit_grad = (jnp.exp(seed_logits - log_total) - onehot) / SEEDS
    weighted = (ppr_weight[:, :, None] * logit_grad[:, None, :]).astype(jnp.bfloat16).reshape(SEEDS * K, C)
    grad_third = jnp.dot(second_act.T, weighted, preferred_element_type=jnp.float32)
    second_grad = jnp.where(second_pre > 0, jnp.dot(weighted, w_third.T, preferred_element_type=jnp.float32), 0.0).astype(jnp.bfloat16)
    grad_second = jnp.dot(first_act.T, second_grad, preferred_element_type=jnp.float32)
    first_grad = jnp.where(first_pre > 0, jnp.dot(second_grad, w_second.T, preferred_element_type=jnp.float32), 0.0).astype(jnp.bfloat16)
    grad_first = jnp.dot(row_block.T, first_grad, preferred_element_type=jnp.float32)
    return loss, seed_logits, grad_first, grad_second, grad_third
```

```python
import functools

import jax
import jax.numpy as jnp
from jax import lax
from jax.experimental import pallas as pl
from jax.experimental.pallas import tpu as pltpu
from jax.sharding import Mesh
from jax.sharding import PartitionSpec as P

CHIPS = ("nodes_0", "nodes_1", "nodes_2")
CORE = "nodes_3"
NODES = (*CHIPS, CORE)
LANES = 128
VMEM_BYTES = 48 << 20

bf16 = jnp.bfloat16
f32 = jnp.float32
i32 = jnp.int32


def iota(shape, dim):
    return lax.broadcasted_iota(i32, shape, dim)


def dot(a, b, over=((1,), (0,))):
    return lax.dot_general(a, b, (over, ((), ())), preferred_element_type=f32)


def whole(shape=None):
    return pl.BlockSpec(memory_space=pltpu.VMEM)


def call(body, outs, ins, scratch=()):
    return pl.pallas_call(
        body,
        out_shape=outs,
        in_specs=ins,
        out_specs=jax.tree.map(lambda _: whole(), outs),
        scratch_shapes=scratch,
        compiler_params=pltpu.CompilerParams(vmem_limit_bytes=VMEM_BYTES),
    )


def request_body(capacity, owner_ref, local_ref, table_ref, earlier_ref):
    owner, local = owner_ref[...], local_ref[...]
    seeds, neighbours = owner.shape
    groups = table_ref.shape[0]
    lane = iota((seeds, groups), 1)
    named = jnp.zeros((seeds, groups), f32)
    wanted = jnp.zeros((seeds, groups), i32)
    for k in range(neighbours):
        hit = owner[:, k : k + 1] == lane
        named = jnp.where(hit, 1.0, named)
        wanted = jnp.where(hit, local[:, k : k + 1], wanted)
    before = (iota((seeds, seeds), 1) < iota((seeds, seeds), 0)).astype(f32)
    earlier = dot(before.astype(bf16), named.astype(bf16))
    earlier_ref[...] = earlier
    place = jnp.where(named > 0, earlier.astype(i32), -1)
    slot = iota((capacity, groups), 0)
    table = jnp.zeros((capacity, groups), i32)
    for s in range(seeds):
        table = jnp.where(place[s : s + 1, :] == slot, wanted[s : s + 1, :], table)
    spare = jnp.zeros((LANES - capacity, groups), i32)
    table_ref[...] = jnp.concatenate([table, spare], axis=0).T


def widen_body(rows_ref, wide_ref):
    wide_ref[...] = rows_ref[...].astype(f32)


def widen(features):
    rows, width = features.shape
    block = 2048
    return pl.pallas_call(
        widen_body,
        grid=(rows // block,),
        out_shape=jax.ShapeDtypeStruct((rows, width), f32),
        in_specs=[pl.BlockSpec((block, width), lambda i: (i, 0))],
        out_specs=pl.BlockSpec((block, width), lambda i: (i, 0)),
        compiler_params=pltpu.CompilerParams(vmem_limit_bytes=VMEM_BYTES),
    )(features)


def pick_body(capacity, owner_t_ref, earlier_ref, pick_ref):
    neighbours, seeds = owner_t_ref.shape
    groups = earlier_ref.shape[1]
    owner_t = owner_t_ref[...]
    lane = iota((neighbours, groups), 1)
    slots = iota((neighbours, groups * capacity), 1)
    for s in range(seeds):
        owner = owner_t[:, s : s + 1]
        place = jnp.sum(jnp.where(owner == lane, earlier_ref[s : s + 1, :], 0.0), axis=1, keepdims=True)
        slot = owner * capacity + place.astype(i32)
        pick_ref[s * neighbours : (s + 1) * neighbours, :] = jnp.where(slots == slot, 1.0, 0.0).astype(bf16)


def serve_body(capacity, asked_ref, wide_ref, rows_ref, stage_ref):
    def one(source, carry):
        base = pl.multiple_of(source * capacity, capacity)
        for p in range(capacity):
            stage_ref[pl.ds(base + p, 1), :] = wide_ref[pl.ds(asked_ref[source, p], 1), :]
        rows_ref[pl.ds(base, capacity), :] = stage_ref[pl.ds(base, capacity), :].astype(bf16)
        return carry

    lax.fori_loop(0, asked_ref.shape[0], one, 0)


def step_body(
    total_seeds,
    core_ref,
    pick_ref,
    arrived_ref,
    weight_ref,
    labels_ref,
    first_ref,
    second_ref,
    third_t_ref,
    logits_ref,
    keep_ref,
    send_ref,
    grads_ref,
):
    seeds, classes = logits_ref.shape
    rows = pick_ref.shape[0]
    neighbours = rows // seeds
    features, hidden = first_ref.shape
    half = keep_ref.shape[0]
    x = dot(pick_ref[...], arrived_ref[...]).astype(bf16)
    first_pre = dot(x, first_ref[...])
    first_act = jnp.maximum(first_pre, 0.0).astype(bf16)
    second_pre = dot(first_act, second_ref[...])
    second_act = jnp.maximum(second_pre, 0.0).astype(bf16)
    row_logits = dot(second_act, third_t_ref[...], ((1,), (1,)))
    weight = weight_ref[...]
    scaled = (weight * row_logits).reshape(seeds, neighbours, classes)
    logits = jnp.sum(scaled, axis=1)
    logits_ref[...] = logits
    highest = jnp.max(logits, axis=1, keepdims=True)
    log_total = jnp.log(jnp.sum(jnp.exp(logits - highest), axis=1, keepdims=True)) + highest
    onehot = jnp.where(labels_ref[...] == iota((seeds, classes), 1), 1.0, 0.0)
    terms = log_total - jnp.sum(onehot * logits, axis=1, keepdims=True)
    logit_grad = (jnp.exp(logits - log_total) - onehot) / total_seeds
    spread = jnp.broadcast_to(logit_grad[:, None, :], (seeds, neighbours, classes)).reshape(rows, classes)
    weighted = (weight * spread).astype(bf16)
    end_first = features
    end_second = end_first + hidden
    end_third = end_second + classes
    grads_ref[end_second:end_third, :] = dot(weighted, second_act, ((0,), (0,)))
    second_grad = jnp.where(second_pre > 0, dot(weighted, third_t_ref[...]), 0.0).astype(bf16)
    grads_ref[end_first:end_second, :] = dot(first_act, second_grad, ((0,), (0,)))
    first_grad = jnp.where(first_pre > 0, dot(second_grad, second_ref[...], ((1,), (1,))), 0.0).astype(bf16)
    grads_ref[:end_first, :] = dot(x, first_grad, ((0,), (0,)))
    grads_ref[end_third:, :] = jnp.zeros((2 * half - end_third, hidden), f32)
    diagonal = iota((seeds, LANES), 0) == iota((seeds, LANES), 1)
    grads_ref[end_third : end_third + 1, :LANES] = jnp.sum(jnp.where(diagonal, terms, 0.0), axis=0, keepdims=True)
    core = core_ref[0]
    keep_ref[...] = grads_ref[pl.ds(pl.multiple_of(core * half, half), half), :]
    send_ref[...] = grads_ref[pl.ds(pl.multiple_of((1 - core) * half, half), half), :].astype(bf16)


def finish_body(total_seeds, core_ref, own_ref, other_ref, loss_ref, first_ref, second_ref, third_t_ref):
    half = own_ref.shape[0]
    end_first = first_ref.shape[0]
    end_second = end_first + second_ref.shape[0]
    end_third = end_second + third_t_ref.shape[0]

    def write(low_ref, high_ref):
        first_ref[...] = low_ref[:end_first, :].astype(f32)
        second_ref[: half - end_first, :] = low_ref[end_first:, :].astype(f32)
        second_ref[half - end_first :, :] = high_ref[: end_second - half, :].astype(f32)
        third_t_ref[...] = high_ref[end_second - half : end_third - half, :].astype(f32)
        terms = high_ref[end_third - half : end_third - half + 1, :LANES].astype(f32)
        loss_ref[...] = jnp.sum(terms, axis=1, keepdims=True) / total_seeds

    @pl.when(core_ref[0] == 0)
    def _():
        write(own_ref, other_ref)

    @pl.when(core_ref[0] != 0)
    def _():
        write(other_ref, own_ref)


def everywhere(parts, axis):
    return lax.all_to_all(parts, axis, 0, 0, tiled=True)


def on_device(features, nbr_owner, nbr_local, ppr_weight, labels, w_first, w_second, w_third):
    groups = lax.axis_size(NODES)
    chips = lax.axis_size(CHIPS)
    seeds, neighbours = nbr_owner.shape
    capacity = min(seeds, 2 * seeds * neighbours // groups)
    width, hidden = w_first.shape
    classes = w_third.shape[1]
    total_seeds = float(seeds * groups)
    vmem = whole()
    smem = pl.BlockSpec(memory_space=pltpu.SMEM)
    shape = jax.ShapeDtypeStruct
    core = lax.axis_index(CORE).astype(i32).reshape(1)
    swap = [(0, 1), (1, 0)]

    table, earlier = call(
        functools.partial(request_body, capacity),
        (shape((groups, LANES), i32), shape((seeds, groups), f32)),
        [vmem, vmem],
    )(nbr_owner, nbr_local)
    asked = everywhere(table.reshape(groups, 1, LANES), NODES).reshape(groups, LANES)
    wide = widen(features)
    (pick,) = call(
        functools.partial(pick_body, capacity),
        (shape((seeds * neighbours, groups * capacity), bf16),),
        [vmem, vmem],
    )(nbr_owner.T, earlier)
    (served,) = call(
        functools.partial(serve_body, capacity),
        (shape((groups * capacity, width), bf16),),
        [smem, vmem],
        [pltpu.VMEM((groups * capacity, width), f32)],
    )(asked, wide)
    arrived = everywhere(served.reshape(groups, capacity, width), NODES).reshape(groups * capacity, width)

    tile = 8
    half = chips * tile * -(-(width + hidden + classes + 1) // (2 * chips * tile))
    seed_logits, keep, send = call(
        functools.partial(step_body, total_seeds),
        (shape((seeds, classes), f32), shape((half, hidden), f32), shape((half, hidden), bf16)),
        [smem] + [vmem] * 7,
        [pltpu.VMEM((2 * half, hidden), f32)],
    )(
        core,
        pick,
        arrived,
        ppr_weight.reshape(-1, 1),
        labels.reshape(-1, 1),
        w_first,
        w_second,
        w_third.T,
    )
    near = lax.ppermute(send, CORE, swap)
    parts = (keep + near.astype(f32)).astype(bf16).reshape(chips, half // chips, hidden)
    mine = jnp.sum(everywhere(parts, CHIPS).astype(f32), axis=0).astype(bf16)
    own = everywhere(jnp.broadcast_to(mine[None], parts.shape), CHIPS).reshape(half, hidden)
    other = lax.ppermute(own, CORE, swap)
    loss, grad_first, grad_second, grad_third_t = call(
        functools.partial(finish_body, total_seeds),
        (
            shape((1, 1), f32),
            shape((width, hidden), f32),
            shape((hidden, hidden), f32),
            shape((classes, hidden), f32),
        ),
        [smem, vmem, vmem],
    )(core, own, other)
    return (loss.reshape(()), seed_logits, grad_first, grad_second, grad_third_t.T)


def solution(mesh):
    finer = Mesh(mesh.devices.reshape(4, 4, 4, 2), NODES)
    placed = (
        P(NODES, None),
        P(NODES, None),
        P(NODES, None),
        P(NODES, None),
        P(NODES),
        P(),
        P(),
        P(),
    )
    return jax.shard_map(
        on_device,
        mesh=finer,
        in_specs=placed,
        out_specs=(P(), P(NODES, None), P(), P(), P()),
        check_vma=False,
    )
```

```python
import functools

import jax
import jax.numpy as jnp
from jax import lax
from jax.experimental import pallas as pl
from jax.experimental.pallas import tpu as pltpu
from jax.sharding import Mesh
from jax.sharding import PartitionSpec as P

CHIPS = ("nodes_0", "nodes_1", "nodes_2")
CORE = "nodes_3"
NODES = (*CHIPS, CORE)
LANES = 128

bf16 = jnp.bfloat16
f32 = jnp.float32
i32 = jnp.int32


def iota(shape, dim):
    return lax.broadcasted_iota(i32, shape, dim)


def dot(a, b, over=((1,), (0,))):
    return lax.dot_general(a, b, (over, ((), ())), preferred_element_type=f32)


VMEM = pl.BlockSpec(memory_space=pltpu.VMEM)
SMEM = pl.BlockSpec(memory_space=pltpu.SMEM)
FAR = pl.BlockSpec(memory_space=pltpu.HBM)


def call(body, outs, ins, scratch=(), megabytes=8, where=VMEM):
    return pl.pallas_call(
        body,
        out_shape=outs,
        in_specs=ins,
        out_specs=jax.tree.map(lambda _: where, outs),
        scratch_shapes=scratch,
        compiler_params=pltpu.CompilerParams(vmem_limit_bytes=megabytes << 20),
    )


def places(capacity, groups, owner, local=None):
    seeds, neighbours = owner.shape
    lane = iota((seeds, groups), 1)
    named = jnp.zeros((seeds, groups), f32)
    wanted = jnp.zeros((seeds, groups), i32)
    for k in range(neighbours):
        hit = owner[:, k : k + 1] == lane
        named = jnp.where(hit, 1.0, named)
        if local is not None:
            wanted = jnp.where(hit, local[:, k : k + 1], wanted)
    before = (iota((seeds, seeds), 1) < iota((seeds, seeds), 0)).astype(f32)
    earlier = dot(before.astype(bf16), named.astype(bf16)).astype(i32)
    return named > 0, earlier, wanted


def request_body(capacity, owner_hbm, local_hbm, table_ref, owner_ref, local_ref, arrivals):
    copies = [
        pltpu.make_async_copy(owner_hbm, owner_ref, arrivals.at[0]),
        pltpu.make_async_copy(local_hbm, local_ref, arrivals.at[1]),
    ]
    for copy in copies:
        copy.start()
    for copy in copies:
        copy.wait()
    groups = table_ref.shape[0]
    seeds = owner_ref.shape[0]
    named, earlier, wanted = places(capacity, groups, owner_ref[...], local_ref[...])
    place = jnp.where(named, earlier, -1)
    slot = iota((capacity, groups), 0)
    table = jnp.zeros((capacity, groups), i32)
    for s in range(seeds):
        table = jnp.where(place[s : s + 1, :] == slot, wanted[s : s + 1, :], table)
    spare = jnp.zeros((LANES - capacity, groups), i32)
    table_ref[...] = jnp.concatenate([table, spare], axis=0).T


def coded_slots(slot):
    return ((128 + (slot & 127)) * (1 << (slot >> 7))).astype(f32)


def hold_body(pairs_hbm, held_ref, arrival):
    copy = pltpu.make_async_copy(pairs_hbm.at[pl.ds(0, held_ref.shape[0])], held_ref, arrival)
    copy.start()
    copy.wait()


def spread_body(capacity, groups, owner_ref, weight_ref, codes_ref, weights_ref):
    seeds, neighbours = owner_ref.shape
    _, earlier, _ = places(capacity, groups, owner_ref[...])
    code_of = coded_slots(iota((seeds, groups), 1) * capacity + earlier)
    owner_t = owner_ref[...].T
    weight_t = weight_ref[...].T
    lane = iota((neighbours, groups), 1)
    for s in range(seeds):
        rows = pl.ds(s * neighbours, neighbours)
        own = jnp.where(owner_t[:, s : s + 1] == lane, code_of[s : s + 1, :], 0.0)
        code = jnp.sum(own, axis=1, keepdims=True)
        codes_ref[rows, :] = jnp.broadcast_to(code, (neighbours, codes_ref.shape[1])).astype(bf16)
        weights_ref[rows, :] = jnp.broadcast_to(weight_t[:, s : s + 1], (neighbours, weights_ref.shape[1]))


def serve_body(
    capacity, asked_ref, held_ref, pairs_hbm, rows_hbm, rows_ref, pairs_ref, stage_ref, turned_ref, index_ref, arrivals, leaving
):
    held, pairs = held_ref.shape[0], pairs_ref.shape[0]
    rest = pl.ds(held, pairs - held)
    near = pltpu.make_async_copy(held_ref, pairs_ref.at[pl.ds(0, held)], arrivals.at[0])
    far = pltpu.make_async_copy(pairs_hbm.at[rest], pairs_ref.at[rest], arrivals.at[1])
    far.start()
    near.start()
    asked = asked_ref[...].T[:capacity, :]
    turned_ref[...] = asked >> 1
    odd = (asked & 1).astype(f32)
    index = pltpu.make_async_copy(turned_ref, index_ref, arrivals.at[2])
    index.start()
    index.wait()
    near.wait()
    far.wait()
    sources = asked.shape[1]
    together = stage_ref.shape[0] // (2 * capacity)

    def some(step, carry):
        for j in range(together):
            source = step * together + j
            low = 2 * j * capacity
            for p in range(capacity):
                stage_ref[low + 2 * p : low + 2 * p + 2, :] = pairs_ref[index_ref[p, source]].astype(f32)
            later = jnp.broadcast_to(pltpu.roll(odd, sources - source, 1)[:, 0:1], (capacity, stage_ref.shape[1])) > 0
            first = stage_ref[pl.ds(low, capacity, stride=2), :]
            second = stage_ref[pl.ds(low + 1, capacity, stride=2), :]
            base = pl.multiple_of(source * capacity, capacity)
            rows_ref[pl.ds(base, capacity), :] = jnp.where(later, second, first).astype(bf16)
        out(step).start()
        return carry

    def out(step):
        size = together * capacity
        span = pl.ds(pl.multiple_of(step * size, size), size)
        return pltpu.make_async_copy(rows_ref.at[span], rows_hbm.at[span], leaving.at[step])

    def last(step, carry):
        out(step).wait()
        return carry

    lax.fori_loop(0, sources // together, some, 0)
    lax.fori_loop(0, sources // together, last, 0)


def step_body(
    total_seeds,
    blocks,
    core_ref,
    codes_ref,
    arrived_ref,
    weights_ref,
    labels_ref,
    first_hbm,
    second_hbm,
    third_t_hbm,
    logits_ref,
    keep_ref,
    send_ref,
    grads_ref,
    first_ref,
    second_ref,
    third_t_ref,
    arrivals,
):
    sources = (first_hbm, second_hbm, third_t_hbm)
    targets = (first_ref, second_ref, third_t_ref)
    copies = [pltpu.make_async_copy(a, b, arrivals.at[i]) for i, (a, b) in enumerate(zip(sources, targets))]
    for copy in copies:
        copy.start()
    seeds, classes = logits_ref.shape
    rows = codes_ref.shape[0]
    neighbours = rows // seeds
    features, hidden = first_ref.shape
    half = keep_ref.shape[0]
    zero = jnp.zeros((), bf16)
    own_rows = [slice(b * rows // blocks, (b + 1) * rows // blocks) for b in range(blocks)]
    own_seeds = [slice(b * seeds // blocks, (b + 1) * seeds // blocks) for b in range(blocks)]
    size, seed_size = rows // blocks, seeds // blocks

    def rectified(pre):
        return jnp.maximum(pre.astype(bf16), zero)

    def masked(act, grad):
        return jnp.where(act > zero, grad.astype(bf16), zero)

    def joined(parts):
        return jnp.concatenate(parts, axis=0)

    slots = arrived_ref.shape[0]
    every_code = coded_slots(iota((16, slots), 1)).astype(bf16)
    every_code = jnp.concatenate([every_code] * (size // 16), axis=0)
    x = []
    for r in own_rows:
        code = jnp.concatenate([codes_ref[r, :]] * (slots // LANES), axis=1)
        pick = jnp.where(code == every_code, jnp.ones((), bf16), zero)
        x.append(dot(pick, arrived_ref[...]).astype(bf16))
    copies[0].wait()
    first_act = [rectified(dot(part, first_ref[...])) for part in x]
    copies[1].wait()
    copies[2].wait()
    second_act = [rectified(dot(part, second_ref[...])) for part in first_act]
    weighted, terms = [], []
    for act, r, s in zip(second_act, own_rows, own_seeds):
        row_logits = dot(act, third_t_ref[...], ((1,), (1,)))
        weight = weights_ref[r, :]
        weight = jnp.concatenate([weight, weight[:, : classes - LANES]], axis=1)
        logits = jnp.sum((weight * row_logits).reshape(seed_size, neighbours, classes), axis=1)
        logits_ref[s, :] = logits
        highest = jnp.max(logits, axis=1, keepdims=True)
        log_total = jnp.log(jnp.sum(jnp.exp(logits - highest), axis=1, keepdims=True)) + highest
        onehot = jnp.where(labels_ref[s, :] == iota((seed_size, classes), 1), 1.0, 0.0)
        terms.append(log_total - jnp.sum(onehot * logits, axis=1, keepdims=True))
        logit_grad = (jnp.exp(logits - log_total) - onehot) / total_seeds
        every = jnp.broadcast_to(logit_grad[:, None, :], (seed_size, neighbours, classes)).reshape(size, classes)
        weighted.append((weight * every).astype(bf16))
    second_grad = [masked(a, dot(g, third_t_ref[...])) for a, g in zip(second_act, weighted)]
    first_grad = [masked(a, dot(g, second_ref[...], ((1,), (1,)))) for a, g in zip(first_act, second_grad)]
    end_first = features
    end_second = end_first + hidden
    end_third = end_second + classes
    down = ((0,), (0,))
    grads_ref[end_second:end_third, :] = dot(joined(weighted), joined(second_act), down)
    grads_ref[end_first:end_second, :] = dot(joined(first_act), joined(second_grad), down)
    grads_ref[:end_first, :] = dot(joined(x), joined(first_grad), down)
    grads_ref[end_third:, :] = jnp.zeros((2 * half - end_third, hidden), f32)
    diagonal = iota((seeds, LANES), 0) == iota((seeds, LANES), 1)
    grads_ref[end_third : end_third + 1, :LANES] = jnp.sum(jnp.where(diagonal, joined(terms), 0.0), axis=0, keepdims=True)
    core = core_ref[0]
    keep_ref[...] = grads_ref[pl.ds(pl.multiple_of(core * half, half), half), :]
    send_ref[...] = grads_ref[pl.ds(pl.multiple_of((1 - core) * half, half), half), :].astype(bf16)


def finish_body(total_seeds, core_ref, own_ref, other_ref, loss_ref, first_ref, second_ref, third_t_ref):
    half = own_ref.shape[0]
    end_first = first_ref.shape[0]
    end_second = end_first + second_ref.shape[0]
    end_third = end_second + third_t_ref.shape[0]

    def write(low_ref, high_ref):
        first_ref[...] = low_ref[:end_first, :].astype(f32)
        second_ref[: half - end_first, :] = low_ref[end_first:, :].astype(f32)
        second_ref[half - end_first :, :] = high_ref[: end_second - half, :].astype(f32)
        third_t_ref[...] = high_ref[end_second - half : end_third - half, :].astype(f32)
        terms = high_ref[end_third - half : end_third - half + 1, :LANES].astype(f32)
        loss_ref[...] = jnp.sum(terms, axis=1, keepdims=True) / total_seeds

    @pl.when(core_ref[0] == 0)
    def _():
        write(own_ref, other_ref)

    @pl.when(core_ref[0] != 0)
    def _():
        write(other_ref, own_ref)


def everywhere(parts, axis):
    return lax.all_to_all(parts, axis, 0, 0, tiled=True)


def on_device(features, nbr_owner, nbr_local, ppr_weight, labels, w_first, w_second, w_third):
    groups = lax.axis_size(NODES)
    chips = lax.axis_size(CHIPS)
    seeds, neighbours = nbr_owner.shape
    capacity = min(seeds, 2 * seeds * neighbours // groups)
    width, hidden = w_first.shape
    classes = w_third.shape[1]
    total_seeds = float(seeds * groups)
    slots = groups * capacity
    shape = jax.ShapeDtypeStruct
    core = lax.axis_index(CORE).astype(i32).reshape(1)
    swap = [(0, 1), (1, 0)]

    table = call(
        functools.partial(request_body, capacity),
        shape((groups, LANES), i32),
        [FAR, FAR],
        [
            pltpu.VMEM((seeds, neighbours), i32),
            pltpu.VMEM((seeds, neighbours), i32),
            pltpu.SemaphoreType.DMA((2,)),
        ],
    )(*(pltpu.with_memory_space_constraint(a, pltpu.HBM) for a in (nbr_owner, nbr_local)))
    asked = everywhere(table.reshape(groups, 1, LANES), NODES).reshape(groups, LANES)
    pairs = pltpu.with_memory_space_constraint(features.reshape(-1, 2, width), pltpu.HBM)
    held = call(
        hold_body,
        pltpu.VMEM((pairs.shape[0] * 3 // 4, 2, width), bf16),
        [FAR],
        [pltpu.SemaphoreType.DMA],
    )(pairs)
    codes, weights = call(
        functools.partial(spread_body, capacity, groups),
        (shape((seeds * neighbours, LANES), bf16), shape((seeds * neighbours, LANES), f32)),
        [VMEM] * 2,
    )(nbr_owner, ppr_weight)
    served = call(
        functools.partial(serve_body, capacity),
        pltpu.HBM((slots, width), bf16),
        [VMEM, VMEM, FAR],
        [
            pltpu.VMEM((slots, width), bf16),
            pltpu.VMEM(pairs.shape, bf16),
            pltpu.VMEM((8 * 2 * capacity, width), f32),
            pltpu.VMEM((capacity, groups), i32),
            pltpu.SMEM((capacity, groups), i32),
            pltpu.SemaphoreType.DMA((3,)),
            pltpu.SemaphoreType.DMA((groups // 8,)),
        ],
        16,
        FAR,
    )(asked, held, pairs)
    arrived = everywhere(served.reshape(groups, capacity, width), NODES).reshape(slots, width)

    tile = 8
    half = chips * tile * -(-(width + hidden + classes + 1) // (2 * chips * tile))
    params = [pltpu.with_memory_space_constraint(p, pltpu.HBM) for p in (w_first, w_second, w_third.T)]
    seed_logits, keep, send = call(
        functools.partial(step_body, total_seeds, 2),
        (shape((seeds, classes), f32), shape((half, hidden), f32), shape((half, hidden), bf16)),
        [SMEM] + [VMEM] * 4 + [FAR] * 3,
        [
            pltpu.VMEM((2 * half, hidden), f32),
            *(pltpu.VMEM(p.shape, p.dtype) for p in params),
            pltpu.SemaphoreType.DMA((3,)),
        ],
        24,
    )(core, codes, arrived, weights, labels.reshape(-1, 1), *params)
    near = lax.ppermute(send, CORE, swap)
    parts = (keep + near.astype(f32)).astype(bf16).reshape(chips, half // chips, hidden)
    mine = jnp.sum(everywhere(parts, CHIPS).astype(f32), axis=0).astype(bf16)
    own = everywhere(jnp.broadcast_to(mine[None], parts.shape), CHIPS).reshape(half, hidden)
    other = lax.ppermute(own, CORE, swap)
    loss, grad_first, grad_second, grad_third_t = call(
        functools.partial(finish_body, total_seeds),
        (
            shape((1, 1), f32),
            shape((width, hidden), f32),
            shape((hidden, hidden), f32),
            shape((classes, hidden), f32),
        ),
        [SMEM, VMEM, VMEM],
    )(core, own, other)
    return (loss.reshape(()), seed_logits, grad_first, grad_second, grad_third_t.T)


def solution(mesh):
    finer = Mesh(mesh.devices.reshape(4, 4, 4, 2), NODES)
    placed = (
        P(NODES, None),
        P(NODES, None),
        P(NODES, None),
        P(NODES, None),
        P(NODES),
        P(),
        P(),
        P(),
    )
    return jax.shard_map(
        on_device,
        mesh=finer,
        in_specs=placed,
        out_specs=(P(), P(NODES, None), P(), P(), P()),
        check_vma=False,
    )
```

```python
import functools

import jax
import jax.numpy as jnp
from jax import lax
from jax.experimental import pallas as pl
from jax.experimental.pallas import tpu as pltpu
from jax.sharding import Mesh
from jax.sharding import PartitionSpec as P

CHIPS = ("nodes_0", "nodes_1", "nodes_2")
CORE = "nodes_3"
NODES = (*CHIPS, CORE)
LANES = 128

bf16 = jnp.bfloat16
f32 = jnp.float32
i32 = jnp.int32


def iota(shape, dim):
    return lax.broadcasted_iota(i32, shape, dim)


def dot(a, b, over=((1,), (0,))):
    return lax.dot_general(a, b, (over, ((), ())), preferred_element_type=f32)


VMEM = pl.BlockSpec(memory_space=pltpu.VMEM)
SMEM = pl.BlockSpec(memory_space=pltpu.SMEM)
FAR = pl.BlockSpec(memory_space=pltpu.HBM)


def call(body, outs, ins, scratch=(), megabytes=8, where=VMEM):
    return pl.pallas_call(
        body,
        out_shape=outs,
        in_specs=ins,
        out_specs=jax.tree.map(lambda _: where, outs),
        scratch_shapes=scratch,
        compiler_params=pltpu.CompilerParams(vmem_limit_bytes=megabytes << 20),
    )


def places(capacity, groups, owner, local=None):
    seeds, neighbours = owner.shape
    lane = iota((seeds, groups), 1)
    named = jnp.zeros((seeds, groups), f32)
    wanted = jnp.zeros((seeds, groups), i32)
    for k in range(neighbours):
        hit = owner[:, k : k + 1] == lane
        named = jnp.where(hit, 1.0, named)
        if local is not None:
            wanted = jnp.where(hit, local[:, k : k + 1], wanted)
    before = (iota((seeds, seeds), 1) < iota((seeds, seeds), 0)).astype(f32)
    earlier = dot(before.astype(bf16), named.astype(bf16)).astype(i32)
    return named > 0, earlier, wanted


def request_body(capacity, owner_hbm, local_hbm, table_ref, owner_ref, local_ref, arrivals):
    copies = [
        pltpu.make_async_copy(owner_hbm, owner_ref, arrivals.at[0]),
        pltpu.make_async_copy(local_hbm, local_ref, arrivals.at[1]),
    ]
    for copy in copies:
        copy.start()
    for copy in copies:
        copy.wait()
    groups = table_ref.shape[0]
    seeds = owner_ref.shape[0]
    named, earlier, wanted = places(capacity, groups, owner_ref[...], local_ref[...])
    place = jnp.where(named, earlier, -1)
    slot = iota((capacity, groups), 0)
    table = jnp.zeros((capacity, groups), i32)
    for s in range(seeds):
        table = jnp.where(place[s : s + 1, :] == slot, wanted[s : s + 1, :], table)
    spare = jnp.zeros((LANES - capacity, groups), i32)
    table_ref[...] = jnp.concatenate([table, spare], axis=0).T


def coded_slots(slot):
    return ((128 + (slot & 127)) * (1 << (slot >> 7))).astype(f32)


def hold_body(pairs_hbm, held_ref, arrival):
    copy = pltpu.make_async_copy(pairs_hbm.at[pl.ds(0, held_ref.shape[0])], held_ref, arrival)
    copy.start()
    copy.wait()


def spread_body(capacity, groups, owner_ref, weight_ref, second_hbm, codes_ref, weights_ref, second_ref, arrival):
    second = pltpu.make_async_copy(second_hbm, second_ref, arrival)
    second.start()
    seeds, neighbours = owner_ref.shape
    _, earlier, _ = places(capacity, groups, owner_ref[...])
    code_of = coded_slots(iota((seeds, groups), 1) * capacity + earlier)
    owner_t = owner_ref[...].T
    weight_t = weight_ref[...].T
    lane = iota((neighbours, groups), 1)
    for s in range(seeds):
        rows = pl.ds(s * neighbours, neighbours)
        own = jnp.where(owner_t[:, s : s + 1] == lane, code_of[s : s + 1, :], 0.0)
        code = jnp.sum(own, axis=1, keepdims=True)
        codes_ref[rows, :] = jnp.broadcast_to(code, (neighbours, codes_ref.shape[1])).astype(bf16)
        weights_ref[rows, :] = jnp.broadcast_to(weight_t[:, s : s + 1], (neighbours, weights_ref.shape[1]))
    second.wait()


def serve_body(
    capacity, asked_ref, held_ref, pairs_hbm, rows_hbm, rows_ref, pairs_ref, stage_ref, turned_ref, index_ref, arrivals, leaving
):
    held, pairs = held_ref.shape[0], pairs_ref.shape[0]
    rest = pl.ds(held, pairs - held)
    near = pltpu.make_async_copy(held_ref, pairs_ref.at[pl.ds(0, held)], arrivals.at[0])
    far = pltpu.make_async_copy(pairs_hbm.at[rest], pairs_ref.at[rest], arrivals.at[1])
    far.start()
    near.start()
    asked = asked_ref[...].T[:capacity, :]
    turned_ref[...] = asked >> 1
    odd = (asked & 1).astype(f32)
    index = pltpu.make_async_copy(turned_ref, index_ref, arrivals.at[2])
    index.start()
    index.wait()
    near.wait()
    far.wait()
    sources = asked.shape[1]
    together = stage_ref.shape[0] // (2 * capacity)

    def some(step, carry):
        for j in range(together):
            source = step * together + j
            low = 2 * j * capacity
            for p in range(capacity):
                stage_ref[low + 2 * p : low + 2 * p + 2, :] = pairs_ref[index_ref[p, source]].astype(f32)
            later = jnp.broadcast_to(pltpu.roll(odd, sources - source, 1)[:, 0:1], (capacity, stage_ref.shape[1])) > 0
            first = stage_ref[pl.ds(low, capacity, stride=2), :]
            second = stage_ref[pl.ds(low + 1, capacity, stride=2), :]
            base = pl.multiple_of(source * capacity, capacity)
            rows_ref[pl.ds(base, capacity), :] = jnp.where(later, second, first).astype(bf16)
        out(step).start()
        return carry

    def out(step):
        size = together * capacity
        span = pl.ds(pl.multiple_of(step * size, size), size)
        return pltpu.make_async_copy(rows_ref.at[span], rows_hbm.at[span], leaving.at[step])

    def last(step, carry):
        out(step).wait()
        return carry

    lax.fori_loop(0, sources // together, some, 0)
    lax.fori_loop(0, sources // together, last, 0)


def step_body(
    total_seeds,
    blocks,
    core_ref,
    codes_ref,
    arrived_ref,
    weights_ref,
    labels_ref,
    first_ref,
    second_ref,
    third_t_ref,
    logits_ref,
    send_ref,
    terms_ref,
    x_ref,
    first_act_ref,
    weighted_ref,
    second_act_ref,
    second_grad_ref,
    first_grad_ref,
    grads_ref,
):
    seeds, classes = logits_ref.shape
    rows = codes_ref.shape[0]
    neighbours = rows // seeds
    zero = jnp.zeros((), bf16)
    own_rows = [slice(b * rows // blocks, (b + 1) * rows // blocks) for b in range(blocks)]
    own_seeds = [slice(b * seeds // blocks, (b + 1) * seeds // blocks) for b in range(blocks)]
    size, seed_size = rows // blocks, seeds // blocks

    def rectified(pre):
        return jnp.maximum(pre.astype(bf16), zero)

    def masked(act, grad):
        return jnp.where(act > zero, grad.astype(bf16), zero)

    def halves(ref, parts):
        wide = ref.shape[2]
        for part, r in zip(parts, own_rows):
            for h in range(2):
                ref[h, r, :] = part[:, h * wide : (h + 1) * wide]

    slots = arrived_ref.shape[0]
    every_code = coded_slots(iota((16, slots), 1)).astype(bf16)
    every_code = jnp.concatenate([every_code] * (size // 16), axis=0)
    x = []
    for r in own_rows:
        code = jnp.concatenate([codes_ref[r, :]] * (slots // LANES), axis=1)
        pick = jnp.where(code == every_code, jnp.ones((), bf16), zero)
        x.append(dot(pick, arrived_ref[...]).astype(bf16))
        x_ref[r, :] = x[-1]
    first_act = [rectified(dot(part, first_ref[...])) for part in x]
    second_act = [rectified(dot(part, second_ref[...])) for part in first_act]
    for part, r in zip(first_act, own_rows):
        first_act_ref[r, :] = part
    halves(second_act_ref, second_act)
    weighted, terms = [], []
    for act, r, s in zip(second_act, own_rows, own_seeds):
        row_logits = dot(act, third_t_ref[...], ((1,), (1,)))
        weight = weights_ref[r, :]
        weight = jnp.concatenate([weight, weight[:, : classes - LANES]], axis=1)
        logits = jnp.sum((weight * row_logits).reshape(seed_size, neighbours, classes), axis=1)
        logits_ref[s, :] = logits
        highest = jnp.max(logits, axis=1, keepdims=True)
        log_total = jnp.log(jnp.sum(jnp.exp(logits - highest), axis=1, keepdims=True)) + highest
        onehot = jnp.where(labels_ref[s, :] == iota((seed_size, classes), 1), 1.0, 0.0)
        terms.append(log_total - jnp.sum(onehot * logits, axis=1, keepdims=True))
        logit_grad = (jnp.exp(logits - log_total) - onehot) / total_seeds
        every = jnp.broadcast_to(logit_grad[:, None, :], (seed_size, neighbours, classes)).reshape(size, classes)
        weighted.append((weight * every).astype(bf16))
        weighted_ref[r, :] = weighted[-1]
    second_grad = [masked(a, dot(g, third_t_ref[...])) for a, g in zip(second_act, weighted)]
    halves(second_grad_ref, second_grad)
    first_grad = [masked(a, dot(g, second_ref[...], ((1,), (1,)))) for a, g in zip(first_act, second_grad)]
    halves(first_grad_ref, first_grad)
    diagonal = iota((seeds, LANES), 0) == iota((seeds, LANES), 1)
    loss_row = jnp.sum(jnp.where(diagonal, jnp.concatenate(terms, axis=0), 0.0), axis=0, keepdims=True)
    terms_ref[...] = jnp.broadcast_to(loss_row, terms_ref.shape)
    other = 1 - core_ref[0]
    write_half(
        grads_ref, loss_row, x_ref, first_act_ref, weighted_ref, second_act_ref, second_grad_ref, first_grad_ref, other
    )
    send_ref[...] = grads_ref[...].astype(bf16)


def write_half(out_ref, loss_row, x_ref, first_act_ref, weighted_ref, second_act_ref, second_grad_ref, first_grad_ref, half):
    down = ((0,), (0,))
    first = dot(x_ref[...], first_grad_ref[half], down)
    second = dot(first_act_ref[...], second_grad_ref[half], down)
    third = dot(weighted_ref[...], second_act_ref[half], down)
    parts = first.shape[1] // LANES
    tall = out_ref.shape[0] // parts
    for j in range(parts):
        at = j * tall
        for piece in (first, second, third):
            out_ref[at : at + piece.shape[0], :] = piece[:, j * LANES : (j + 1) * LANES]
            at += piece.shape[0]
        out_ref[at : (j + 1) * tall, :] = jnp.zeros(((j + 1) * tall - at, LANES), f32)
        out_ref[at : at + 1, :] = loss_row


def keep_body(
    core_ref, terms_ref, x_ref, first_act_ref, weighted_ref, second_act_ref, second_grad_ref, first_grad_ref, keep_ref
):
    write_half(
        keep_ref,
        terms_ref[:1, :],
        x_ref,
        first_act_ref,
        weighted_ref,
        second_act_ref,
        second_grad_ref,
        first_grad_ref,
        core_ref[0],
    )


def total_body(chips, parts_ref, total_ref):
    rows = parts_ref.shape[0]
    chunk = rows // chips
    tall = -(-chunk // 8) * 8
    column = iota((tall, rows), 1)
    which = ((column.astype(f32) + 0.5) / chunk).astype(i32)
    same = jnp.where(column - which * chunk == iota((tall, rows), 0), 1.0, 0.0).astype(bf16)
    total = dot(same, parts_ref[...]).astype(bf16)
    total_ref[...] = dot(same, total, ((0,), (0,))).astype(bf16)


def columns(half, half_ref, outs, stages, arrivals):
    copies = []
    at = 0
    for i, (out, stage) in enumerate(zip(outs, stages)):
        size, wide = stage.shape
        parts = wide // LANES
        tall = half_ref.shape[0] // parts
        for j in range(parts):
            stage[:, j * LANES : (j + 1) * LANES] = half_ref[j * tall + at : j * tall + at + size, :].astype(f32)
        span = pl.ds(pl.multiple_of(half * wide, wide), wide)
        copies.append(pltpu.make_async_copy(stage, out.at[:, span], arrivals.at[i]))
        copies[-1].start()
        at += size
    for copy in copies:
        copy.wait()


def own_body(core_ref, own_ref, first_hbm, second_hbm, third_t_hbm, *scratch):
    columns(core_ref[0], own_ref, (first_hbm, second_hbm, third_t_hbm), scratch[:3], scratch[3])


def other_body(
    total_seeds,
    core_ref,
    own_ref,
    other_ref,
    given_first,
    given_second,
    given_third_t,
    loss_ref,
    first_hbm,
    second_hbm,
    third_t_hbm,
    *scratch,
):
    del given_first, given_second, given_third_t
    outs = (first_hbm, second_hbm, third_t_hbm)
    at = sum(out.shape[0] for out in outs)
    low = jnp.where(core_ref[0] == 0, own_ref[at : at + 1, :].astype(f32), other_ref[at : at + 1, :].astype(f32))
    loss_ref[...] = jnp.sum(low, axis=1, keepdims=True) / total_seeds
    columns(1 - core_ref[0], other_ref, outs, scratch[:3], scratch[3])


def everywhere(parts, axis):
    return lax.all_to_all(parts, axis, 0, 0, tiled=True)


def on_device(features, nbr_owner, nbr_local, ppr_weight, labels, w_first, w_second, w_third):
    groups = lax.axis_size(NODES)
    chips = lax.axis_size(CHIPS)
    seeds, neighbours = nbr_owner.shape
    capacity = min(seeds, 2 * seeds * neighbours // groups)
    width, hidden = w_first.shape
    classes = w_third.shape[1]
    total_seeds = float(seeds * groups)
    slots = groups * capacity
    shape = jax.ShapeDtypeStruct
    core = lax.axis_index(CORE).astype(i32).reshape(1)
    swap = [(0, 1), (1, 0)]

    table = call(
        functools.partial(request_body, capacity),
        shape((groups, LANES), i32),
        [FAR, FAR],
        [
            pltpu.VMEM((seeds, neighbours), i32),
            pltpu.VMEM((seeds, neighbours), i32),
            pltpu.SemaphoreType.DMA((2,)),
        ],
    )(*(pltpu.with_memory_space_constraint(a, pltpu.HBM) for a in (nbr_owner, nbr_local)))
    asked = everywhere(table.reshape(groups, 1, LANES), NODES).reshape(groups, LANES)
    pairs = pltpu.with_memory_space_constraint(features.reshape(-1, 2, width), pltpu.HBM)
    held = call(
        hold_body,
        pltpu.VMEM((pairs.shape[0] * 3 // 4, 2, width), bf16),
        [FAR],
        [pltpu.SemaphoreType.DMA],
    )(pairs)
    codes, weights, second = call(
        functools.partial(spread_body, capacity, groups),
        (
            shape((seeds * neighbours, LANES), bf16),
            shape((seeds * neighbours, LANES), f32),
            pltpu.VMEM(w_second.shape, bf16),
        ),
        [VMEM, VMEM, FAR],
        [pltpu.SemaphoreType.DMA],
    )(nbr_owner, ppr_weight, pltpu.with_memory_space_constraint(w_second, pltpu.HBM))
    served = call(
        functools.partial(serve_body, capacity),
        pltpu.HBM((slots, width), bf16),
        [VMEM, VMEM, FAR],
        [
            pltpu.VMEM((slots, width), bf16),
            pltpu.VMEM(pairs.shape, bf16),
            pltpu.VMEM((8 * 2 * capacity, width), f32),
            pltpu.VMEM((capacity, groups), i32),
            pltpu.SMEM((capacity, groups), i32),
            pltpu.SemaphoreType.DMA((3,)),
            pltpu.SemaphoreType.DMA((groups // 8,)),
        ],
        16,
        FAR,
    )(asked, held, pairs)
    arrived = everywhere(served.reshape(groups, capacity, width), NODES).reshape(slots, width)

    rows = seeds * neighbours
    half = hidden // 2
    blocks = half // LANES
    tall = 2 * chips // blocks * -(-(width + hidden + classes + 1) * blocks // (2 * chips))
    grads = (blocks * tall, LANES)
    seed_logits, send, *kept = call(
        functools.partial(step_body, total_seeds, 2),
        (
            shape((seeds, classes), f32),
            shape(grads, bf16),
            shape((8, LANES), f32),
            shape((rows, width), bf16),
            shape((rows, hidden), bf16),
            shape((rows, classes), bf16),
            *(shape((2, rows, half), bf16) for _ in range(3)),
        ),
        [SMEM] + [VMEM] * 7,
        [pltpu.VMEM(grads, f32)],
        32,
    )(core, codes, arrived, weights, labels.reshape(-1, 1), w_first, second, w_third.T)
    near = lax.ppermute(send, CORE, swap)
    keep = call(keep_body, shape(grads, f32), [SMEM] + [VMEM] * 7, (), 16)(core, *kept)
    parts = (keep + near.astype(f32)).astype(bf16)
    mine = everywhere(parts.reshape(-1, 2, LANES), CHIPS).reshape(grads)
    totals = call(functools.partial(total_body, chips), shape(grads, bf16), [VMEM])(mine)
    own = everywhere(totals.reshape(-1, 2, LANES), CHIPS).reshape(grads)
    other = lax.ppermute(own, CORE, swap)
    sizes = (width, hidden, classes)
    scratch = [*(pltpu.VMEM((n, half), f32) for n in sizes), pltpu.SemaphoreType.DMA((3,))]
    sums = tuple(pltpu.HBM((n, hidden), f32) for n in sizes)
    started = call(own_body, sums, [SMEM, VMEM], scratch, 8, FAR)(core, own)
    loss, grad_first, grad_second, grad_third_t = pl.pallas_call(
        functools.partial(other_body, total_seeds),
        out_shape=(shape((1, 1), f32), *sums),
        in_specs=[SMEM, VMEM, VMEM, FAR, FAR, FAR],
        out_specs=(VMEM, FAR, FAR, FAR),
        scratch_shapes=scratch,
        input_output_aliases={3: 1, 4: 2, 5: 3},
        compiler_params=pltpu.CompilerParams(vmem_limit_bytes=8 << 20),
    )(core, own, other, *started)
    return (loss.reshape(()), seed_logits, grad_first, grad_second, grad_third_t.T)


def solution(mesh):
    finer = Mesh(mesh.devices.reshape(4, 4, 4, 2), NODES)
    placed = (
        P(NODES, None),
        P(NODES, None),
        P(NODES, None),
        P(NODES, None),
        P(NODES),
        P(),
        P(),
        P(),
    )
    return jax.shard_map(
        on_device,
        mesh=finer,
        in_specs=placed,
        out_specs=(P(), P(NODES, None), P(), P(), P()),
        check_vma=False,
    )
```

```python
import functools

import jax
import jax.numpy as jnp
from jax import lax
from jax.experimental import pallas as pl
from jax.experimental.pallas import tpu as pltpu
from jax.sharding import Mesh
from jax.sharding import PartitionSpec as P

CHIPS = ("nodes_0", "nodes_1", "nodes_2")
CORE = "nodes_3"
NODES = (*CHIPS, CORE)
LANES = 128

bf16 = jnp.bfloat16
f32 = jnp.float32
i32 = jnp.int32


def iota(shape, dim):
    return lax.broadcasted_iota(i32, shape, dim)


def dot(a, b, over=((1,), (0,))):
    return lax.dot_general(a, b, (over, ((), ())), preferred_element_type=f32)


VMEM = pl.BlockSpec(memory_space=pltpu.VMEM)
SMEM = pl.BlockSpec(memory_space=pltpu.SMEM)
FAR = pl.BlockSpec(memory_space=pltpu.HBM)


def call(body, outs, ins, scratch=(), megabytes=8, where=VMEM):
    return pl.pallas_call(
        body,
        out_shape=outs,
        in_specs=ins,
        out_specs=jax.tree.map(lambda _: where, outs),
        scratch_shapes=scratch,
        compiler_params=pltpu.CompilerParams(vmem_limit_bytes=megabytes << 20),
    )


def places(capacity, groups, owner, local=None):
    seeds, neighbours = owner.shape
    lane = iota((seeds, groups), 1)
    named = jnp.zeros((seeds, groups), f32)
    wanted = jnp.zeros((seeds, groups), i32)
    for k in range(neighbours):
        hit = owner[:, k : k + 1] == lane
        named = jnp.where(hit, 1.0, named)
        if local is not None:
            wanted = jnp.where(hit, local[:, k : k + 1], wanted)
    before = (iota((seeds, seeds), 1) < iota((seeds, seeds), 0)).astype(f32)
    earlier = dot(before.astype(bf16), named.astype(bf16)).astype(i32)
    return named > 0, earlier, wanted


def request_body(capacity, owner_hbm, local_hbm, table_ref, owner_ref, local_ref, arrivals):
    copies = [
        pltpu.make_async_copy(owner_hbm, owner_ref, arrivals.at[0]),
        pltpu.make_async_copy(local_hbm, local_ref, arrivals.at[1]),
    ]
    for copy in copies:
        copy.start()
    for copy in copies:
        copy.wait()
    groups = table_ref.shape[0]
    seeds = owner_ref.shape[0]
    named, earlier, wanted = places(capacity, groups, owner_ref[...], local_ref[...])
    place = jnp.where(named, earlier, -1)
    slot = iota((capacity, groups), 0)
    table = jnp.zeros((capacity, groups), i32)
    for s in range(seeds):
        table = jnp.where(place[s : s + 1, :] == slot, wanted[s : s + 1, :], table)
    spare = jnp.zeros((LANES - capacity, groups), i32)
    table_ref[...] = jnp.concatenate([table, spare], axis=0).T


def coded_slots(slot):
    return ((128 + (slot & 127)) * (1 << (slot >> 7))).astype(f32)


def hold_body(pairs_hbm, held_ref, arrival):
    copy = pltpu.make_async_copy(pairs_hbm.at[pl.ds(0, held_ref.shape[0])], held_ref, arrival)
    copy.start()
    copy.wait()


def spread_body(capacity, groups, owner_ref, weight_ref, second_hbm, codes_ref, weights_ref, second_ref, arrival):
    second = pltpu.make_async_copy(second_hbm, second_ref, arrival)
    second.start()
    seeds, neighbours = owner_ref.shape
    _, earlier, _ = places(capacity, groups, owner_ref[...])
    code_of = coded_slots(iota((seeds, groups), 1) * capacity + earlier)
    owner_t = owner_ref[...].T
    weight_t = weight_ref[...].T
    lane = iota((neighbours, groups), 1)
    for s in range(seeds):
        rows = pl.ds(s * neighbours, neighbours)
        own = jnp.where(owner_t[:, s : s + 1] == lane, code_of[s : s + 1, :], 0.0)
        code = jnp.sum(own, axis=1, keepdims=True)
        codes_ref[rows, :] = jnp.broadcast_to(code, (neighbours, codes_ref.shape[1])).astype(bf16)
        weights_ref[rows, :] = jnp.broadcast_to(weight_t[:, s : s + 1], (neighbours, weights_ref.shape[1]))
    second.wait()


def serve_body(
    capacity, asked_ref, held_ref, pairs_hbm, rows_hbm, rows_ref, pairs_ref, stage_ref, wide_ref, turned_ref, index_ref, arrivals, leaving
):
    held, pairs = held_ref.shape[0], pairs_ref.shape[0]
    rest = pl.ds(held, pairs - held)
    near = pltpu.make_async_copy(held_ref, pairs_ref.at[pl.ds(0, held)], arrivals.at[0])
    far = pltpu.make_async_copy(pairs_hbm.at[rest], pairs_ref.at[rest], arrivals.at[1])
    far.start()
    near.start()
    asked = asked_ref[...]
    turned_ref[...] = asked.T[:capacity, :] >> 1
    index = pltpu.make_async_copy(turned_ref, index_ref, arrivals.at[2])
    index.start()
    index.wait()
    near.wait()
    far.wait()
    odd = (asked & 1) > 0
    sources, width = asked.shape[0], stage_ref.shape[2]
    together = capacity // leaving.shape[0]
    copies = []
    for group in range(leaving.shape[0]):
        for p in range(group * together, (group + 1) * together):
            stage = stage_ref.at[p % stage_ref.shape[0]]
            for source in range(sources):
                stage[2 * source : 2 * source + 2, :] = pairs_ref[index_ref[p, source]].astype(f32)
            first = stage[pl.ds(0, sources, stride=2), :]
            second = stage[pl.ds(1, sources, stride=2), :]
            at = pl.ds(p - group * together, sources, stride=together)
            wide_ref[group, at, :] = jnp.where(odd[:, p : p + 1], second, first)
        ready = wide_ref[group].reshape(sources, together, width).astype(bf16)
        rows_ref[group] = ready
        span = pl.ds(group * together, together)
        copies.append(pltpu.make_async_copy(rows_ref.at[group], rows_hbm.at[:, span, :], leaving.at[group]))
        copies[-1].start()
    for copy in copies:
        copy.wait()


def step_body(
    total_seeds,
    blocks,
    core_ref,
    codes_ref,
    arrived_ref,
    weights_ref,
    labels_ref,
    first_ref,
    second_ref,
    third_t_ref,
    logits_ref,
    send_ref,
    terms_ref,
    x_ref,
    first_act_ref,
    weighted_ref,
    second_act_ref,
    second_grad_ref,
    first_grad_ref,
    grads_ref,
):
    seeds, classes = logits_ref.shape
    rows = codes_ref.shape[0]
    neighbours = rows // seeds
    zero = jnp.zeros((), bf16)
    own_rows = [slice(b * rows // blocks, (b + 1) * rows // blocks) for b in range(blocks)]
    own_seeds = [slice(b * seeds // blocks, (b + 1) * seeds // blocks) for b in range(blocks)]
    size, seed_size = rows // blocks, seeds // blocks

    def rectified(pre):
        return jnp.maximum(pre.astype(bf16), zero)

    def masked(act, grad):
        return jnp.where(act > zero, grad.astype(bf16), zero)

    def halves(ref, parts):
        wide = ref.shape[2]
        for part, r in zip(parts, own_rows):
            for h in range(2):
                ref[h, r, :] = part[:, h * wide : (h + 1) * wide]

    slots = arrived_ref.shape[0]
    side = slots // 2
    arrived = jnp.concatenate([arrived_ref[:side, :], arrived_ref[side:, :]], axis=1)
    every_code = coded_slots(iota((16, side), 1)).astype(bf16)
    every_code = jnp.concatenate([every_code] * (size // 16), axis=0)
    bound = float(128 << (side >> 7))
    x = []
    for r in own_rows:
        late = codes_ref[r, :] >= jnp.asarray(bound, bf16)
        code = jnp.where(late, codes_ref[r, :] * jnp.asarray(128.0 / bound, bf16), codes_ref[r, :])
        code = jnp.concatenate([code] * (side // LANES), axis=1)
        pick = jnp.where(code == every_code, jnp.ones((), bf16), zero)
        both = dot(pick, arrived).astype(bf16)
        x.append(jnp.where(late, both[:, LANES:], both[:, :LANES]))
        x_ref[r, :] = x[-1]
    first_act = [rectified(dot(part, first_ref[...])) for part in x]
    second_act = [rectified(dot(part, second_ref[...])) for part in first_act]
    for part, r in zip(first_act, own_rows):
        first_act_ref[r, :] = part
    halves(second_act_ref, second_act)
    weighted, terms = [], []
    for act, r, s in zip(second_act, own_rows, own_seeds):
        row_logits = dot(act, third_t_ref[...], ((1,), (1,)))
        weight = weights_ref[r, :]
        weight = jnp.concatenate([weight, weight[:, : classes - LANES]], axis=1)
        logits = jnp.sum((weight * row_logits).reshape(seed_size, neighbours, classes), axis=1)
        logits_ref[s, :] = logits
        highest = jnp.max(logits, axis=1, keepdims=True)
        log_total = jnp.log(jnp.sum(jnp.exp(logits - highest), axis=1, keepdims=True)) + highest
        onehot = jnp.where(labels_ref[s, :] == iota((seed_size, classes), 1), 1.0, 0.0)
        terms.append(log_total - jnp.sum(onehot * logits, axis=1, keepdims=True))
        logit_grad = (jnp.exp(logits - log_total) - onehot) / total_seeds
        every = jnp.broadcast_to(logit_grad[:, None, :], (seed_size, neighbours, classes)).reshape(size, classes)
        weighted.append((weight * every).astype(bf16))
        weighted_ref[r, :] = weighted[-1]
    second_grad = [masked(a, dot(g, third_t_ref[...])) for a, g in zip(second_act, weighted)]
    halves(second_grad_ref, second_grad)
    first_grad = [masked(a, dot(g, second_ref[...], ((1,), (1,)))) for a, g in zip(first_act, second_grad)]
    halves(first_grad_ref, first_grad)
    diagonal = iota((seeds, LANES), 0) == iota((seeds, LANES), 1)
    loss_row = jnp.sum(jnp.where(diagonal, jnp.concatenate(terms, axis=0), 0.0), axis=0, keepdims=True)
    terms_ref[...] = jnp.broadcast_to(loss_row, terms_ref.shape)
    other = 1 - core_ref[0]
    write_half(
        grads_ref, loss_row, x_ref, first_act_ref, weighted_ref, second_act_ref, second_grad_ref, first_grad_ref, other
    )
    send_ref[...] = grads_ref[...].astype(bf16)


def write_half(out_ref, loss_row, x_ref, first_act_ref, weighted_ref, second_act_ref, second_grad_ref, first_grad_ref, half):
    down = ((0,), (0,))
    first = dot(x_ref[...], first_grad_ref[half], down)
    second = dot(first_act_ref[...], second_grad_ref[half], down)
    third = dot(weighted_ref[...], second_act_ref[half], down)
    parts = first.shape[1] // LANES
    tall = out_ref.shape[0] // parts
    for j in range(parts):
        at = j * tall
        for piece in (first, second, third):
            out_ref[at : at + piece.shape[0], :] = piece[:, j * LANES : (j + 1) * LANES]
            at += piece.shape[0]
        out_ref[at : (j + 1) * tall, :] = jnp.zeros(((j + 1) * tall - at, LANES), f32)
        out_ref[at : at + 1, :] = loss_row


def keep_body(
    core_ref, terms_ref, x_ref, first_act_ref, weighted_ref, second_act_ref, second_grad_ref, first_grad_ref, keep_ref
):
    write_half(
        keep_ref,
        terms_ref[:1, :],
        x_ref,
        first_act_ref,
        weighted_ref,
        second_act_ref,
        second_grad_ref,
        first_grad_ref,
        core_ref[0],
    )


def total_body(chips, parts_ref, total_ref):
    rows = parts_ref.shape[0]
    chunk = rows // chips
    tall = -(-chunk // 8) * 8
    column = iota((tall, rows), 1)
    which = ((column.astype(f32) + 0.5) / chunk).astype(i32)
    same = jnp.where(column - which * chunk == iota((tall, rows), 0), 1.0, 0.0).astype(bf16)
    total = dot(same, parts_ref[...]).astype(bf16)
    total_ref[...] = dot(same, total, ((0,), (0,))).astype(bf16)


def columns(half, half_ref, outs, stages, arrivals):
    copies = []
    at = 0
    for i, (out, stage) in enumerate(zip(outs, stages)):
        size, wide = stage.shape
        parts = wide // LANES
        tall = half_ref.shape[0] // parts
        for j in range(parts):
            stage[:, j * LANES : (j + 1) * LANES] = half_ref[j * tall + at : j * tall + at + size, :].astype(f32)
        span = pl.ds(pl.multiple_of(half * wide, wide), wide)
        copies.append(pltpu.make_async_copy(stage, out.at[:, span], arrivals.at[i]))
        copies[-1].start()
        at += size
    for copy in copies:
        copy.wait()


def own_body(core_ref, own_ref, first_hbm, second_hbm, third_t_hbm, *scratch):
    columns(core_ref[0], own_ref, (first_hbm, second_hbm, third_t_hbm), scratch[:3], scratch[3])


def other_body(
    total_seeds,
    core_ref,
    own_ref,
    other_ref,
    given_first,
    given_second,
    given_third_t,
    loss_ref,
    first_hbm,
    second_hbm,
    third_t_hbm,
    *scratch,
):
    del given_first, given_second, given_third_t
    outs = (first_hbm, second_hbm, third_t_hbm)
    at = sum(out.shape[0] for out in outs)
    low = jnp.where(core_ref[0] == 0, own_ref[at : at + 1, :].astype(f32), other_ref[at : at + 1, :].astype(f32))
    loss_ref[...] = jnp.sum(low, axis=1, keepdims=True) / total_seeds
    columns(1 - core_ref[0], other_ref, outs, scratch[:3], scratch[3])


def everywhere(parts, axis):
    return lax.all_to_all(parts, axis, 0, 0, tiled=True)


def on_device(features, nbr_owner, nbr_local, ppr_weight, labels, w_first, w_second, w_third):
    groups = lax.axis_size(NODES)
    chips = lax.axis_size(CHIPS)
    seeds, neighbours = nbr_owner.shape
    capacity = min(seeds, 2 * seeds * neighbours // groups)
    width, hidden = w_first.shape
    classes = w_third.shape[1]
    total_seeds = float(seeds * groups)
    slots = groups * capacity
    shape = jax.ShapeDtypeStruct
    core = lax.axis_index(CORE).astype(i32).reshape(1)
    swap = [(0, 1), (1, 0)]

    table = call(
        functools.partial(request_body, capacity),
        shape((groups, LANES), i32),
        [FAR, FAR],
        [
            pltpu.VMEM((seeds, neighbours), i32),
            pltpu.VMEM((seeds, neighbours), i32),
            pltpu.SemaphoreType.DMA((2,)),
        ],
    )(*(pltpu.with_memory_space_constraint(a, pltpu.HBM) for a in (nbr_owner, nbr_local)))
    asked = everywhere(table.reshape(groups, 1, LANES), NODES).reshape(groups, LANES)
    pairs = pltpu.with_memory_space_constraint(features.reshape(-1, 2, width), pltpu.HBM)
    held = call(
        hold_body,
        pltpu.VMEM((pairs.shape[0] * 3 // 4, 2, width), bf16),
        [FAR],
        [pltpu.SemaphoreType.DMA],
    )(pairs)
    codes, weights, second = call(
        functools.partial(spread_body, capacity, groups),
        (
            shape((seeds * neighbours, LANES), bf16),
            shape((seeds * neighbours, LANES), f32),
            pltpu.VMEM(w_second.shape, bf16),
        ),
        [VMEM, VMEM, FAR],
        [pltpu.SemaphoreType.DMA],
    )(nbr_owner, ppr_weight, pltpu.with_memory_space_constraint(w_second, pltpu.HBM))
    served = call(
        functools.partial(serve_body, capacity),
        pltpu.HBM((groups, capacity, width), bf16),
        [VMEM, VMEM, FAR],
        [
            pltpu.VMEM((2, groups, capacity // 2, width), bf16),
            pltpu.VMEM(pairs.shape, bf16),
            pltpu.VMEM((2, 2 * groups, width), f32),
            pltpu.VMEM((2, groups * capacity // 2, width), f32),
            pltpu.VMEM((capacity, groups), i32),
            pltpu.SMEM((capacity, groups), i32),
            pltpu.SemaphoreType.DMA((3,)),
            pltpu.SemaphoreType.DMA((2,)),
        ],
        16,
        FAR,
    )(asked, held, pairs)
    arrived = everywhere(served, NODES).reshape(slots, width)

    rows = seeds * neighbours
    half = hidden // 2
    blocks = half // LANES
    tall = 2 * chips // blocks * -(-(width + hidden + classes + 1) * blocks // (2 * chips))
    grads = (blocks * tall, LANES)
    seed_logits, send, *kept = call(
        functools.partial(step_body, total_seeds, 2),
        (
            shape((seeds, classes), f32),
            shape(grads, bf16),
            shape((8, LANES), f32),
            shape((rows, width), bf16),
            shape((rows, hidden), bf16),
            shape((rows, classes), bf16),
            *(shape((2, rows, half), bf16) for _ in range(3)),
        ),
        [SMEM] + [VMEM] * 7,
        [pltpu.VMEM(grads, f32)],
        32,
    )(core, codes, arrived, weights, labels.reshape(-1, 1), w_first, second, w_third.T)
    near = lax.ppermute(send, CORE, swap)
    keep = call(keep_body, shape(grads, f32), [SMEM] + [VMEM] * 7, (), 16)(core, *kept)
    parts = (keep + near.astype(f32)).astype(bf16)
    mine = everywhere(parts.reshape(-1, 2, LANES), CHIPS).reshape(grads)
    totals = call(functools.partial(total_body, chips), shape(grads, bf16), [VMEM])(mine)
    own = everywhere(totals.reshape(-1, 2, LANES), CHIPS).reshape(grads)
    other = lax.ppermute(own, CORE, swap)
    sizes = (width, hidden, classes)
    scratch = [*(pltpu.VMEM((n, half), f32) for n in sizes), pltpu.SemaphoreType.DMA((3,))]
    sums = tuple(pltpu.HBM((n, hidden), f32) for n in sizes)
    started = call(own_body, sums, [SMEM, VMEM], scratch, 8, FAR)(core, own)
    loss, grad_first, grad_second, grad_third_t = pl.pallas_call(
        functools.partial(other_body, total_seeds),
        out_shape=(shape((1, 1), f32), *sums),
        in_specs=[SMEM, VMEM, VMEM, FAR, FAR, FAR],
        out_specs=(VMEM, FAR, FAR, FAR),
        scratch_shapes=scratch,
        input_output_aliases={3: 1, 4: 2, 5: 3},
        compiler_params=pltpu.CompilerParams(vmem_limit_bytes=8 << 20),
    )(core, own, other, *started)
    return (loss.reshape(()), seed_logits, grad_first, grad_second, grad_third_t.T)


def solution(mesh):
    finer = Mesh(mesh.devices.reshape(4, 4, 4, 2), NODES)
    placed = (
        P(NODES, None),
        P(NODES, None),
        P(NODES, None),
        P(NODES, None),
        P(NODES),
        P(),
        P(),
        P(),
    )
    return jax.shard_map(
        on_device,
        mesh=finer,
        in_specs=placed,
        out_specs=(P(), P(NODES, None), P(), P(), P()),
        check_vma=False,
    )
```

```python
import functools

import jax
import jax.numpy as jnp
from jax import lax
from jax.experimental import pallas as pl
from jax.experimental.pallas import tpu as pltpu
from jax.sharding import Mesh
from jax.sharding import PartitionSpec as P

CHIPS = ("nodes_0", "nodes_1", "nodes_2")
CORE = "nodes_3"
NODES = (*CHIPS, CORE)
LANES = 128

bf16 = jnp.bfloat16
f32 = jnp.float32
i32 = jnp.int32


def iota(shape, dim):
    return lax.broadcasted_iota(i32, shape, dim)


def dot(a, b, over=((1,), (0,))):
    return lax.dot_general(a, b, (over, ((), ())), preferred_element_type=f32)


VMEM = pl.BlockSpec(memory_space=pltpu.VMEM)
SMEM = pl.BlockSpec(memory_space=pltpu.SMEM)
FAR = pl.BlockSpec(memory_space=pltpu.HBM)


def call(body, outs, ins, scratch=(), megabytes=8, where=VMEM, aliases=()):
    return pl.pallas_call(
        body,
        out_shape=outs,
        in_specs=ins,
        out_specs=where if isinstance(where, tuple) else jax.tree.map(lambda _: where, outs),
        input_output_aliases=dict(aliases),
        scratch_shapes=scratch,
        compiler_params=pltpu.CompilerParams(vmem_limit_bytes=megabytes << 20),
    )


def places(capacity, groups, owner, local=None):
    seeds, neighbours = owner.shape
    lane = iota((seeds, groups), 1)
    named = jnp.zeros((seeds, groups), f32)
    wanted = jnp.zeros((seeds, groups), i32)
    for k in range(neighbours):
        hit = owner[:, k : k + 1] == lane
        named = jnp.where(hit, 1.0, named)
        if local is not None:
            wanted = jnp.where(hit, local[:, k : k + 1], wanted)
    before = (iota((seeds, seeds), 1) < iota((seeds, seeds), 0)).astype(f32)
    earlier = dot(before.astype(bf16), named.astype(bf16)).astype(i32)
    return named > 0, earlier, wanted


def request_body(capacity, owner_hbm, local_hbm, pairs_hbm, table_ref, pairs_ref, owner_ref, local_ref, arrivals):
    copies = [
        pltpu.make_async_copy(owner_hbm, owner_ref, arrivals.at[0]),
        pltpu.make_async_copy(local_hbm, local_ref, arrivals.at[1]),
    ]
    for copy in copies:
        copy.start()
    pairs = pltpu.make_async_copy(pairs_hbm, pairs_ref, arrivals.at[2])
    pairs.start()
    for copy in copies:
        copy.wait()
    groups = table_ref.shape[0]
    seeds = owner_ref.shape[0]
    named, earlier, wanted = places(capacity, groups, owner_ref[...], local_ref[...])
    place = jnp.where(named, earlier, -1)
    slot = iota((capacity, groups), 0)
    table = jnp.zeros((capacity, groups), i32)
    for s in range(seeds):
        table = jnp.where(place[s : s + 1, :] == slot, wanted[s : s + 1, :], table)
    spare = jnp.zeros((LANES - capacity, groups), i32)
    table_ref[...] = jnp.concatenate([table, spare], axis=0).T
    pairs.wait()


def coded_slots(slot):
    return ((128 + (slot & 127)) * (1 << (slot >> 7))).astype(f32)


def spread_body(capacity, groups, owner_ref, weight_ref, second_hbm, codes_ref, weights_ref, second_ref, arrival):
    second = pltpu.make_async_copy(second_hbm, second_ref, arrival)
    second.start()
    seeds, neighbours = owner_ref.shape
    _, earlier, _ = places(capacity, groups, owner_ref[...])
    code_of = coded_slots(iota((seeds, groups), 1) * capacity + earlier)
    owner_t = owner_ref[...].T
    weight_t = weight_ref[...].T
    lane = iota((neighbours, groups), 1)
    for s in range(seeds):
        rows = pl.ds(s * neighbours, neighbours)
        own = jnp.where(owner_t[:, s : s + 1] == lane, code_of[s : s + 1, :], 0.0)
        code = jnp.sum(own, axis=1, keepdims=True)
        codes_ref[rows, :] = jnp.broadcast_to(code, (neighbours, codes_ref.shape[1])).astype(bf16)
        weights_ref[rows, :] = jnp.broadcast_to(weight_t[:, s : s + 1], (neighbours, weights_ref.shape[1]))
    second.wait()


def serve_body(
    capacity, asked_ref, pairs_ref, rows_hbm, rows_ref, stage_ref, wide_ref, turned_ref, index_ref, arrival, leaving
):
    asked = asked_ref[...]
    turned_ref[...] = asked.T[:capacity, :] >> 1
    index = pltpu.make_async_copy(turned_ref, index_ref, arrival)
    index.start()
    index.wait()
    odd = (asked & 1) > 0
    groups = leaving.shape[0]
    size = asked.shape[0] // groups
    copies = []
    for group in range(groups):
        span = slice(group * size, (group + 1) * size)
        for p in range(capacity):
            stage = stage_ref.at[p % stage_ref.shape[0]]
            for source in range(size):
                stage[2 * source : 2 * source + 2, :] = pairs_ref[index_ref[p, span.start + source]].astype(f32)
            first = stage[pl.ds(0, size, stride=2), :]
            second = stage[pl.ds(1, size, stride=2), :]
            wide_ref[group, pl.ds(p, size, stride=capacity), :] = jnp.where(odd[span, p : p + 1], second, first)
        rows_ref[span] = wide_ref[group].reshape(size, capacity, -1).astype(bf16)
        copies.append(pltpu.make_async_copy(rows_ref.at[span], rows_hbm.at[span], leaving.at[group]))
        copies[-1].start()
    for copy in copies:
        copy.wait()


def step_body(
    total_seeds,
    blocks,
    core_ref,
    codes_ref,
    arrived_ref,
    weights_ref,
    labels_ref,
    first_ref,
    second_ref,
    third_t_ref,
    logits_hbm,
    send_ref,
    terms_ref,
    x_ref,
    first_act_ref,
    weighted_ref,
    second_act_ref,
    second_grad_ref,
    first_grad_ref,
    grads_ref,
    logits_ref,
    leaving,
):
    seeds, classes = logits_ref.shape
    rows = codes_ref.shape[0]
    neighbours = rows // seeds
    zero = jnp.zeros((), bf16)
    own_rows = [slice(b * rows // blocks, (b + 1) * rows // blocks) for b in range(blocks)]
    own_seeds = [slice(b * seeds // blocks, (b + 1) * seeds // blocks) for b in range(blocks)]
    size, seed_size = rows // blocks, seeds // blocks

    def rectified(pre):
        return jnp.maximum(pre.astype(bf16), zero)

    def masked(act, grad):
        return jnp.where(act > zero, grad.astype(bf16), zero)

    def halves(ref, parts):
        wide = ref.shape[2]
        for part, r in zip(parts, own_rows):
            for h in range(2):
                ref[h, r, :] = part[:, h * wide : (h + 1) * wide]

    slots = arrived_ref.shape[0]
    side = slots // 2
    arrived = jnp.concatenate([arrived_ref[:side, :], arrived_ref[side:, :]], axis=1)
    every_code = coded_slots(iota((16, side), 1)).astype(bf16)
    every_code = jnp.concatenate([every_code] * (size // 16), axis=0)
    bound = float(128 << (side >> 7))
    x = []
    for r in own_rows:
        late = codes_ref[r, :] >= jnp.asarray(bound, bf16)
        code = jnp.where(late, codes_ref[r, :] * jnp.asarray(128.0 / bound, bf16), codes_ref[r, :])
        code = jnp.concatenate([code] * (side // LANES), axis=1)
        pick = jnp.where(code == every_code, jnp.ones((), bf16), zero)
        both = dot(pick, arrived).astype(bf16)
        x.append(jnp.where(late, both[:, LANES:], both[:, :LANES]))
        x_ref[r, :] = x[-1]
    first_act = [rectified(dot(part, first_ref[...])) for part in x]
    second_act = [rectified(dot(part, second_ref[...])) for part in first_act]
    for part, r in zip(first_act, own_rows):
        first_act_ref[r, :] = part
    halves(second_act_ref, second_act)
    weighted, terms = [], []
    for act, r, s in zip(second_act, own_rows, own_seeds):
        row_logits = dot(act, third_t_ref[...], ((1,), (1,)))
        weight = weights_ref[r, :]
        weight = jnp.concatenate([weight, weight[:, : classes - LANES]], axis=1)
        logits = jnp.sum((weight * row_logits).reshape(seed_size, neighbours, classes), axis=1)
        logits_ref[s, :] = logits
        highest = jnp.max(logits, axis=1, keepdims=True)
        log_total = jnp.log(jnp.sum(jnp.exp(logits - highest), axis=1, keepdims=True)) + highest
        onehot = jnp.where(labels_ref[s, :] == iota((seed_size, classes), 1), 1.0, 0.0)
        terms.append(log_total - jnp.sum(onehot * logits, axis=1, keepdims=True))
        logit_grad = (jnp.exp(logits - log_total) - onehot) / total_seeds
        every = jnp.broadcast_to(logit_grad[:, None, :], (seed_size, neighbours, classes)).reshape(size, classes)
        weighted.append((weight * every).astype(bf16))
        weighted_ref[r, :] = weighted[-1]
    logits_copy = pltpu.make_async_copy(logits_ref, logits_hbm, leaving)
    logits_copy.start()
    second_grad = [masked(a, dot(g, third_t_ref[...])) for a, g in zip(second_act, weighted)]
    halves(second_grad_ref, second_grad)
    first_grad = [masked(a, dot(g, second_ref[...], ((1,), (1,)))) for a, g in zip(first_act, second_grad)]
    halves(first_grad_ref, first_grad)
    diagonal = iota((seeds, LANES), 0) == iota((seeds, LANES), 1)
    loss_row = jnp.sum(jnp.where(diagonal, jnp.concatenate(terms, axis=0), 0.0), axis=0, keepdims=True)
    loss_row = loss_row.astype(bf16).astype(f32)
    terms_ref[...] = jnp.broadcast_to(loss_row, terms_ref.shape)
    other = 1 - core_ref[0]
    write_half(
        grads_ref, loss_row, x_ref, first_act_ref, weighted_ref, second_act_ref, second_grad_ref, first_grad_ref, other
    )
    send_ref[...] = grads_ref[...].astype(bf16)
    logits_copy.wait()


def write_half(out_ref, loss_row, x_ref, first_act_ref, weighted_ref, second_act_ref, second_grad_ref, first_grad_ref, half):
    down = ((0,), (0,))
    first = dot(x_ref[...], first_grad_ref[half], down)
    second = dot(first_act_ref[...], second_grad_ref[half], down)
    third = dot(weighted_ref[...], second_act_ref[half], down)
    parts = first.shape[1] // LANES
    tall = out_ref.shape[0] // parts
    for j in range(parts):
        at = j * tall
        for piece in (first, second, third):
            out_ref[at : at + piece.shape[0], :] = piece[:, j * LANES : (j + 1) * LANES]
            at += piece.shape[0]
        out_ref[at : (j + 1) * tall, :] = jnp.zeros(((j + 1) * tall - at, LANES), f32)
        out_ref[at : at + 1, :] = loss_row


def keep_body(
    core_ref, terms_ref, x_ref, first_act_ref, weighted_ref, second_act_ref, second_grad_ref, first_grad_ref, keep_ref
):
    write_half(
        keep_ref,
        terms_ref[:1, :],
        x_ref,
        first_act_ref,
        weighted_ref,
        second_act_ref,
        second_grad_ref,
        first_grad_ref,
        core_ref[0],
    )


def total_body(chips, parts_ref, total_ref):
    rows = parts_ref.shape[0]
    chunk = rows // chips
    tall = -(-chunk // 8) * 8
    column = iota((tall, rows), 1)
    which = ((column.astype(f32) + 0.5) / chunk).astype(i32)
    same = jnp.where(column - which * chunk == iota((tall, rows), 0), 1.0, 0.0).astype(bf16)
    total = dot(same, parts_ref[...]).astype(bf16)
    total_ref[...] = dot(same, total, ((0,), (0,))).astype(bf16)


def columns(half, half_ref, outs, stages, arrivals):
    copies = []
    at = 0
    for i, (out, stage) in enumerate(zip(outs, stages)):
        size, wide = stage.shape
        parts = wide // LANES
        tall = half_ref.shape[0] // parts
        for j in range(parts):
            stage[:, j * LANES : (j + 1) * LANES] = half_ref[j * tall + at : j * tall + at + size, :].astype(f32)
        span = pl.ds(pl.multiple_of(half * wide, wide), wide)
        copies.append(pltpu.make_async_copy(stage, out.at[:, span], arrivals.at[i]))
        copies[-1].start()
        at += size
    for copy in copies:
        copy.wait()


def own_body(total_seeds, core_ref, own_ref, first_hbm, second_hbm, third_t_hbm, loss_ref, *scratch):
    outs = (first_hbm, second_hbm, third_t_hbm)
    at = sum(out.shape[0] for out in outs)
    loss_ref[...] = jnp.sum(own_ref[at : at + 1, :].astype(f32), axis=1, keepdims=True) / total_seeds
    columns(core_ref[0], own_ref, outs, scratch[:3], scratch[3])


def other_body(core_ref, other_ref, given_first, given_second, given_third_t, first_hbm, second_hbm, third_t_hbm, *scratch):
    del given_first, given_second, given_third_t
    columns(1 - core_ref[0], other_ref, (first_hbm, second_hbm, third_t_hbm), scratch[:3], scratch[3])


def everywhere(parts, axis):
    return lax.all_to_all(parts, axis, 0, 0, tiled=True)


def on_device(features, nbr_owner, nbr_local, ppr_weight, labels, w_first, w_second, w_third):
    groups = lax.axis_size(NODES)
    chips = lax.axis_size(CHIPS)
    seeds, neighbours = nbr_owner.shape
    capacity = min(seeds, 2 * seeds * neighbours // groups)
    width, hidden = w_first.shape
    classes = w_third.shape[1]
    total_seeds = float(seeds * groups)
    slots = groups * capacity
    shape = jax.ShapeDtypeStruct
    core = lax.axis_index(CORE).astype(i32).reshape(1)
    swap = [(0, 1), (1, 0)]

    pairs = features.reshape(-1, 2, width)
    table, pairs = call(
        functools.partial(request_body, capacity),
        (shape((groups, LANES), i32), pltpu.VMEM(pairs.shape, bf16)),
        [FAR] * 3,
        [
            pltpu.VMEM((seeds, neighbours), i32),
            pltpu.VMEM((seeds, neighbours), i32),
            pltpu.SemaphoreType.DMA((3,)),
        ],
    )(*(pltpu.with_memory_space_constraint(a, pltpu.HBM) for a in (nbr_owner, nbr_local, pairs)))
    asked = everywhere(table.reshape(groups, 1, LANES), NODES).reshape(groups, LANES)
    codes, weights, second = call(
        functools.partial(spread_body, capacity, groups),
        (
            shape((seeds * neighbours, LANES), bf16),
            shape((seeds * neighbours, LANES), f32),
            pltpu.VMEM(w_second.shape, bf16),
        ),
        [VMEM, VMEM, FAR],
        [pltpu.SemaphoreType.DMA],
    )(nbr_owner, ppr_weight, pltpu.with_memory_space_constraint(w_second, pltpu.HBM))
    served = call(
        functools.partial(serve_body, capacity),
        pltpu.HBM((groups, capacity, width), bf16),
        [VMEM, VMEM],
        [
            pltpu.VMEM((groups, capacity, width), bf16),
            pltpu.VMEM((4, 2 * groups // 4, width), f32),
            pltpu.VMEM((4, groups * capacity // 4, width), f32),
            pltpu.VMEM((capacity, groups), i32),
            pltpu.SMEM((capacity, groups), i32),
            pltpu.SemaphoreType.DMA,
            pltpu.SemaphoreType.DMA((4,)),
        ],
        16,
        FAR,
    )(asked, pairs)
    arrived = everywhere(served, NODES).reshape(slots, width)

    rows = seeds * neighbours
    half = hidden // 2
    blocks = half // LANES
    tall = 2 * chips // blocks * -(-(width + hidden + classes + 1) * blocks // (2 * chips))
    grads = (blocks * tall, LANES)
    seed_logits, send, *kept = call(
        functools.partial(step_body, total_seeds, 2),
        (
            pltpu.HBM((seeds, classes), f32),
            shape(grads, bf16),
            shape((8, LANES), f32),
            shape((rows, width), bf16),
            shape((rows, hidden), bf16),
            shape((rows, classes), bf16),
            *(shape((2, rows, half), bf16) for _ in range(3)),
        ),
        [SMEM] + [VMEM] * 7,
        [pltpu.VMEM(grads, f32), pltpu.VMEM((seeds, classes), f32), pltpu.SemaphoreType.DMA],
        32,
        (FAR, *[VMEM] * 8),
    )(core, codes, arrived, weights, labels.reshape(-1, 1), w_first, second, w_third.T)
    near = lax.ppermute(send, CORE, swap)
    keep = call(keep_body, shape(grads, f32), [SMEM] + [VMEM] * 7, (), 16)(core, *kept)
    parts = (keep + near.astype(f32)).astype(bf16)
    mine = everywhere(parts.reshape(-1, 2, LANES), CHIPS).reshape(grads)
    totals = call(functools.partial(total_body, chips), shape(grads, bf16), [VMEM])(mine)
    own = everywhere(totals.reshape(-1, 2, LANES), CHIPS).reshape(grads)
    other = lax.ppermute(own, CORE, swap)
    sizes = (width, hidden, classes)
    scratch = [*(pltpu.VMEM((n, half), f32) for n in sizes), pltpu.SemaphoreType.DMA((3,))]
    sums = tuple(pltpu.HBM((n, hidden), f32) for n in sizes)
    *started, loss = call(
        functools.partial(own_body, total_seeds),
        (*sums, shape((1, 1), f32)),
        [SMEM, VMEM],
        scratch,
        8,
        (FAR, FAR, FAR, VMEM),
    )(core, own)
    grad_first, grad_second, grad_third_t = call(
        other_body, sums, [SMEM, VMEM, FAR, FAR, FAR], scratch, 8, FAR, {2: 0, 3: 1, 4: 2}
    )(core, other, *started)
    return (loss.reshape(()), seed_logits, grad_first, grad_second, grad_third_t.T)


def solution(mesh):
    finer = Mesh(mesh.devices.reshape(4, 4, 4, 2), NODES)
    placed = (
        P(NODES, None),
        P(NODES, None),
        P(NODES, None),
        P(NODES, None),
        P(NODES),
        P(),
        P(),
        P(),
    )
    return jax.shard_map(
        on_device,
        mesh=finer,
        in_specs=placed,
        out_specs=(P(), P(NODES, None), P(), P(), P()),
        check_vma=False,
    )
```

```python
import functools

import jax
import jax.numpy as jnp
from jax import lax
from jax.experimental import pallas as pl
from jax.experimental.pallas import tpu as pltpu
from jax.sharding import Mesh
from jax.sharding import PartitionSpec as P

CHIPS = ("nodes_0", "nodes_1", "nodes_2")
CORE = "nodes_3"
NODES = (*CHIPS, CORE)
LANES = 128

bf16 = jnp.bfloat16
f32 = jnp.float32
i32 = jnp.int32


def iota(shape, dim):
    return lax.broadcasted_iota(i32, shape, dim)


def dot(a, b, over=((1,), (0,))):
    return lax.dot_general(a, b, (over, ((), ())), preferred_element_type=f32)


VMEM = pl.BlockSpec(memory_space=pltpu.VMEM)
SMEM = pl.BlockSpec(memory_space=pltpu.SMEM)
FAR = pl.BlockSpec(memory_space=pltpu.HBM)


def call(body, outs, ins, scratch=(), megabytes=8, where=VMEM, aliases=()):
    return pl.pallas_call(
        body,
        out_shape=outs,
        in_specs=ins,
        out_specs=where if isinstance(where, tuple) else jax.tree.map(lambda _: where, outs),
        input_output_aliases=dict(aliases),
        scratch_shapes=scratch,
        compiler_params=pltpu.CompilerParams(vmem_limit_bytes=megabytes << 20),
    )


def places(capacity, groups, owner, local):
    seeds, neighbours = owner.shape
    lane = iota((seeds, groups), 1)
    named = jnp.zeros((seeds, groups), f32)
    wanted = jnp.zeros((seeds, groups), i32)
    for k in range(neighbours):
        hit = owner[:, k : k + 1] == lane
        named = jnp.where(hit, 1.0, named)
        wanted = jnp.where(hit, local[:, k : k + 1], wanted)
    before = (iota((seeds, seeds), 1) < iota((seeds, seeds), 0)).astype(f32)
    earlier = dot(before.astype(bf16), named.astype(bf16)).astype(i32)
    return named > 0, earlier, wanted


def request_body(
    capacity,
    core_ref,
    owner_hbm,
    local_hbm,
    weight_hbm,
    labels_hbm,
    pairs_hbm,
    table_ref,
    codes_ref,
    weights_ref,
    onehot_ref,
    pairs_ref,
    owner_ref,
    local_ref,
    weight_ref,
    labels_ref,
    arrivals,
):
    del core_ref
    small = zip((owner_hbm, local_hbm, weight_hbm, labels_hbm), (owner_ref, local_ref, weight_ref, labels_ref))
    copies = [pltpu.make_async_copy(source, target, arrivals.at[i]) for i, (source, target) in enumerate(small)]
    for copy in copies:
        copy.start()
    pairs = pltpu.make_async_copy(pairs_hbm, pairs_ref, arrivals.at[len(copies)])
    pairs.start()
    for copy in copies:
        copy.wait()
    groups = table_ref.shape[0]
    owner = owner_ref[...]
    seeds, neighbours = owner.shape
    named, earlier, wanted = places(capacity, groups, owner, local_ref[...])
    place = jnp.where(named, earlier, -1)
    slot = iota((capacity, groups), 0)
    table = jnp.zeros((capacity, groups), i32)
    for s in range(seeds):
        table = jnp.where(place[s : s + 1, :] == slot, wanted[s : s + 1, :], table)
    spare = jnp.zeros((LANES - capacity, groups), i32)
    table_ref[...] = jnp.concatenate([table, spare], axis=0).T
    code_of = coded_slots(iota((seeds, groups), 1) * capacity + earlier)
    owner_t = owner.T
    weight_t = weight_ref[...].T
    lane = iota((neighbours, groups), 1)
    own = []
    for s in range(seeds):
        own.append(jnp.where(owner_t[:, s : s + 1] == lane, code_of[s : s + 1, :], 0.0).astype(bf16))
        rows = pl.ds(s * neighbours, neighbours)
        weights_ref[rows, :] = jnp.broadcast_to(weight_t[:, s : s + 1], (neighbours, weights_ref.shape[1]))
    everything = jnp.ones((groups, codes_ref.shape[1]), bf16)
    codes_ref[...] = dot(jnp.concatenate(own, axis=0), everything).astype(bf16)
    diagonal = iota((seeds, seeds), 0) == iota((seeds, seeds), 1)
    label = jnp.sum(jnp.where(diagonal, labels_ref[...].astype(f32), 0.0), axis=1, keepdims=True).astype(i32)
    onehot_ref[...] = jnp.where(label == iota(onehot_ref.shape, 1), 1.0, 0.0)
    pairs.wait()


def coded_slots(slot):
    return ((128 + (slot & 127)) * (1 << (slot >> 7))).astype(f32)


def serve_body(
    capacity, asked_ref, pairs_ref, rows_ref, stage_ref, wide_ref, turned_ref, index_ref, arrival
):
    asked = asked_ref[...]
    turned_ref[...] = asked.T[:capacity, :] >> 1
    index = pltpu.make_async_copy(turned_ref, index_ref, arrival)
    index.start()
    index.wait()
    odd = (asked & 1) > 0
    groups = wide_ref.shape[0]
    size = asked.shape[0] // groups
    for group in range(groups):
        span = slice(group * size, (group + 1) * size)
        for p in range(capacity):
            stage = stage_ref.at[p % stage_ref.shape[0]]
            for source in range(size):
                stage[2 * source : 2 * source + 2, :] = pairs_ref[index_ref[p, span.start + source]].astype(f32)
            first = stage[pl.ds(0, size, stride=2), :]
            second = stage[pl.ds(1, size, stride=2), :]
            wide_ref[group, pl.ds(p, size, stride=capacity), :] = jnp.where(odd[span, p : p + 1], second, first)
        rows_ref[span] = wide_ref[group].reshape(size, capacity, -1).astype(bf16)


def step_body(
    total_seeds,
    blocks,
    core_ref,
    codes_ref,
    arrived_ref,
    weights_ref,
    onehot_ref,
    first_ref,
    second_ref,
    third_t_ref,
    logits_hbm,
    send_ref,
    terms_ref,
    x_ref,
    first_act_ref,
    weighted_ref,
    second_act_ref,
    second_grad_ref,
    first_grad_ref,
    grads_ref,
    logits_ref,
    leaving,
):
    seeds, classes = logits_ref.shape
    rows = codes_ref.shape[0]
    neighbours = rows // seeds
    zero = jnp.zeros((), bf16)
    own_rows = [slice(b * rows // blocks, (b + 1) * rows // blocks) for b in range(blocks)]
    own_seeds = [slice(b * seeds // blocks, (b + 1) * seeds // blocks) for b in range(blocks)]
    size, seed_size = rows // blocks, seeds // blocks

    def rectified(pre):
        return jnp.maximum(pre.astype(bf16), zero)

    def masked(act, grad):
        return jnp.where(act > zero, grad.astype(bf16), zero)

    def halves(ref, parts):
        wide = ref.shape[2]
        for part, r in zip(parts, own_rows):
            for h in range(2):
                ref[h, r, :] = part[:, h * wide : (h + 1) * wide]

    slots = arrived_ref.shape[0]
    side = slots // 2
    arrived = jnp.concatenate([arrived_ref[:side, :], arrived_ref[side:, :]], axis=1)
    every_code = coded_slots(iota((16, side), 1)).astype(bf16)
    every_code = jnp.concatenate([every_code] * (size // 16), axis=0)
    bound = float(128 << (side >> 7))
    x = []
    for r in own_rows:
        late = codes_ref[r, :] >= jnp.asarray(bound, bf16)
        code = jnp.where(late, codes_ref[r, :] * jnp.asarray(128.0 / bound, bf16), codes_ref[r, :])
        code = jnp.concatenate([code] * (side // LANES), axis=1)
        pick = jnp.where(code == every_code, jnp.ones((), bf16), zero)
        both = dot(pick, arrived).astype(bf16)
        x.append(jnp.where(late, both[:, LANES:], both[:, :LANES]))
        x_ref[r, :] = x[-1]
    first_act = [rectified(dot(part, first_ref[...])) for part in x]
    second_act = [rectified(dot(part, second_ref[...])) for part in first_act]
    for part, r in zip(first_act, own_rows):
        first_act_ref[r, :] = part
    halves(second_act_ref, second_act)
    weighted, terms = [], []
    for act, r, s in zip(second_act, own_rows, own_seeds):
        row_logits = dot(act, third_t_ref[...], ((1,), (1,)))
        weight = weights_ref[r, :]
        weight = jnp.concatenate([weight, weight[:, : classes - LANES]], axis=1)
        logits = jnp.sum((weight * row_logits).reshape(seed_size, neighbours, classes), axis=1)
        logits_ref[s, :] = logits
        highest = jnp.max(logits, axis=1, keepdims=True)
        log_total = jnp.log(jnp.sum(jnp.exp(logits - highest), axis=1, keepdims=True)) + highest
        onehot = onehot_ref[s, :]
        terms.append(log_total - jnp.sum(onehot * logits, axis=1, keepdims=True))
        logit_grad = (jnp.exp(logits - log_total) - onehot) / total_seeds
        every = jnp.broadcast_to(logit_grad[:, None, :], (seed_size, neighbours, classes)).reshape(size, classes)
        weighted.append((weight * every).astype(bf16))
        weighted_ref[r, :] = weighted[-1]
    logits_copy = pltpu.make_async_copy(logits_ref, logits_hbm, leaving)
    logits_copy.start()
    second_grad = [masked(a, dot(g, third_t_ref[...])) for a, g in zip(second_act, weighted)]
    halves(second_grad_ref, second_grad)
    first_grad = [masked(a, dot(g, second_ref[...], ((1,), (1,)))) for a, g in zip(first_act, second_grad)]
    halves(first_grad_ref, first_grad)
    diagonal = iota((seeds, LANES), 0) == iota((seeds, LANES), 1)
    loss_row = jnp.sum(jnp.where(diagonal, jnp.concatenate(terms, axis=0), 0.0), axis=0, keepdims=True)
    loss_row = loss_row.astype(bf16).astype(f32)
    terms_ref[...] = jnp.broadcast_to(loss_row, terms_ref.shape)
    other = 1 - core_ref[0]
    write_half(
        grads_ref, loss_row, x_ref, first_act_ref, weighted_ref, second_act_ref, second_grad_ref, first_grad_ref, other
    )
    send_ref[...] = grads_ref[...].astype(bf16)
    logits_copy.wait()


def write_half(out_ref, loss_row, x_ref, first_act_ref, weighted_ref, second_act_ref, second_grad_ref, first_grad_ref, half):
    down = ((0,), (0,))
    first = dot(x_ref[...], first_grad_ref[half], down)
    second = dot(first_act_ref[...], second_grad_ref[half], down)
    third = dot(weighted_ref[...], second_act_ref[half], down)
    parts = first.shape[1] // LANES
    tall = out_ref.shape[0] // parts
    for j in range(parts):
        at = j * tall
        for piece in (first, second, third):
            out_ref[at : at + piece.shape[0], :] = piece[:, j * LANES : (j + 1) * LANES]
            at += piece.shape[0]
        out_ref[at : (j + 1) * tall, :] = jnp.zeros(((j + 1) * tall - at, LANES), f32)
        out_ref[at : at + 1, :] = loss_row


def keep_body(
    core_ref, terms_ref, x_ref, first_act_ref, weighted_ref, second_act_ref, second_grad_ref, first_grad_ref, keep_ref
):
    write_half(
        keep_ref,
        terms_ref[:1, :],
        x_ref,
        first_act_ref,
        weighted_ref,
        second_act_ref,
        second_grad_ref,
        first_grad_ref,
        core_ref[0],
    )


def total_body(chips, parts_ref, total_ref):
    rows = parts_ref.shape[0]
    chunk = rows // chips
    tall = -(-chunk // 8) * 8
    column = iota((tall, rows), 1)
    which = ((column.astype(f32) + 0.5) / chunk).astype(i32)
    same = jnp.where(column - which * chunk == iota((tall, rows), 0), 1.0, 0.0).astype(bf16)
    total = dot(same, parts_ref[...]).astype(bf16)
    total_ref[...] = dot(same, total, ((0,), (0,))).astype(bf16)


def columns(half, half_ref, outs, stages, arrivals):
    copies = []
    at = 0
    for i, (out, stage) in enumerate(zip(outs, stages)):
        size, wide = stage.shape
        parts = wide // LANES
        tall = half_ref.shape[0] // parts
        for j in range(parts):
            stage[:, j * LANES : (j + 1) * LANES] = half_ref[j * tall + at : j * tall + at + size, :].astype(f32)
        span = pl.ds(pl.multiple_of(half * wide, wide), wide)
        copies.append(pltpu.make_async_copy(stage, out.at[:, span], arrivals.at[i]))
        copies[-1].start()
        at += size
    for copy in copies:
        copy.wait()


def own_body(total_seeds, core_ref, own_ref, first_hbm, second_hbm, third_t_hbm, loss_ref, *scratch):
    outs = (first_hbm, second_hbm, third_t_hbm)
    at = sum(out.shape[0] for out in outs)
    loss_ref[...] = jnp.sum(own_ref[at : at + 1, :].astype(f32), axis=1, keepdims=True) / total_seeds
    columns(core_ref[0], own_ref, outs, scratch[:3], scratch[3])


def other_body(core_ref, other_ref, given_first, given_second, given_third_t, first_hbm, second_hbm, third_t_hbm, *scratch):
    del given_first, given_second, given_third_t
    columns(1 - core_ref[0], other_ref, (first_hbm, second_hbm, third_t_hbm), scratch[:3], scratch[3])


def everywhere(parts, axis):
    return lax.all_to_all(parts, axis, 0, 0, tiled=True)


def on_device(features, nbr_owner, nbr_local, ppr_weight, labels, w_first, w_second, w_third):
    groups = lax.axis_size(NODES)
    chips = lax.axis_size(CHIPS)
    seeds, neighbours = nbr_owner.shape
    capacity = min(seeds, 2 * seeds * neighbours // groups)
    width, hidden = w_first.shape
    classes = w_third.shape[1]
    total_seeds = float(seeds * groups)
    slots = groups * capacity
    shape = jax.ShapeDtypeStruct
    core = lax.axis_index(CORE).astype(i32).reshape(1)
    swap = [(0, 1), (1, 0)]

    pairs = features.reshape(-1, 2, width)
    rows = seeds * neighbours
    table, codes, weights, onehot, pairs = call(
        functools.partial(request_body, capacity),
        (
            shape((groups, LANES), i32),
            shape((rows, LANES), bf16),
            shape((rows, LANES), f32),
            shape((seeds, classes), f32),
            pltpu.VMEM(pairs.shape, bf16),
        ),
        [SMEM] + [FAR] * 5,
        [
            *(pltpu.VMEM((seeds, neighbours), t) for t in (i32, i32, f32)),
            pltpu.VMEM((1, seeds), i32),
            pltpu.SemaphoreType.DMA((5,)),
        ],
    )(
        core,
        *(
            pltpu.with_memory_space_constraint(a, pltpu.HBM)
            for a in (nbr_owner, nbr_local, ppr_weight, labels.reshape(1, -1), pairs)
        ),
    )
    asked = everywhere(table.reshape(groups, 1, LANES), NODES).reshape(groups, LANES)
    served = call(
        functools.partial(serve_body, capacity),
        shape((groups, capacity, width), bf16),
        [VMEM, VMEM],
        [
            pltpu.VMEM((4, 2 * groups // 4, width), f32),
            pltpu.VMEM((4, groups * capacity // 4, width), f32),
            pltpu.VMEM((capacity, groups), i32),
            pltpu.SMEM((capacity, groups), i32),
            pltpu.SemaphoreType.DMA,
        ],
        16,
    )(asked, pairs)
    arrived = everywhere(served, NODES).reshape(slots, width)

    half = hidden // 2
    blocks = half // LANES
    tall = 2 * chips // blocks * -(-(width + hidden + classes + 1) * blocks // (2 * chips))
    grads = (blocks * tall, LANES)
    seed_logits, send, *kept = call(
        functools.partial(step_body, total_seeds, 2),
        (
            pltpu.HBM((seeds, classes), f32),
            shape(grads, bf16),
            shape((8, LANES), f32),
            shape((rows, width), bf16),
            shape((rows, hidden), bf16),
            shape((rows, classes), bf16),
            *(shape((2, rows, half), bf16) for _ in range(3)),
        ),
        [SMEM] + [VMEM] * 7,
        [pltpu.VMEM(grads, f32), pltpu.VMEM((seeds, classes), f32), pltpu.SemaphoreType.DMA],
        32,
        (FAR, *[VMEM] * 8),
    )(core, codes, arrived, weights, onehot, w_first, w_second, w_third.T)
    near = lax.ppermute(send, CORE, swap)
    keep = call(keep_body, shape(grads, f32), [SMEM] + [VMEM] * 7, (), 16)(core, *kept)
    parts = (keep + near.astype(f32)).astype(bf16)
    mine = everywhere(parts.reshape(-1, 2, LANES), CHIPS).reshape(grads)
    totals = call(functools.partial(total_body, chips), shape(grads, bf16), [VMEM])(mine)
    own = everywhere(totals.reshape(-1, 2, LANES), CHIPS).reshape(grads)
    other = lax.ppermute(own, CORE, swap)
    sizes = (width, hidden, classes)
    scratch = [*(pltpu.VMEM((n, half), f32) for n in sizes), pltpu.SemaphoreType.DMA((3,))]
    sums = tuple(pltpu.HBM((n, hidden), f32) for n in sizes)
    *started, loss = call(
        functools.partial(own_body, total_seeds),
        (*sums, shape((1, 1), f32)),
        [SMEM, VMEM],
        scratch,
        8,
        (FAR, FAR, FAR, VMEM),
    )(core, own)
    grad_first, grad_second, grad_third_t = call(
        other_body, sums, [SMEM, VMEM, FAR, FAR, FAR], scratch, 8, FAR, {2: 0, 3: 1, 4: 2}
    )(core, other, *started)
    return (loss.reshape(()), seed_logits, grad_first, grad_second, grad_third_t.T)


def solution(mesh):
    finer = Mesh(mesh.devices.reshape(4, 4, 4, 2), NODES)
    placed = (
        P(NODES, None),
        P(NODES, None),
        P(NODES, None),
        P(NODES, None),
        P(NODES),
        P(),
        P(),
        P(),
    )
    return jax.shard_map(
        on_device,
        mesh=finer,
        in_specs=placed,
        out_specs=(P(), P(NODES, None), P(), P(), P()),
        check_vma=False,
    )
```

```python
import functools

import jax
import jax.numpy as jnp
from jax import lax
from jax.experimental import pallas as pl
from jax.experimental.pallas import tpu as pltpu
from jax.sharding import Mesh
from jax.sharding import PartitionSpec as P

CHIPS = ("nodes_0", "nodes_1", "nodes_2")
CORE = "nodes_3"
NODES = (*CHIPS, CORE)
LANES = 128

bf16 = jnp.bfloat16
f32 = jnp.float32
i32 = jnp.int32


def iota(shape, dim):
    return lax.broadcasted_iota(i32, shape, dim)


def dot(a, b, over=((1,), (0,))):
    return lax.dot_general(a, b, (over, ((), ())), preferred_element_type=f32)


VMEM = pl.BlockSpec(memory_space=pltpu.VMEM)
SMEM = pl.BlockSpec(memory_space=pltpu.SMEM)
FAR = pl.BlockSpec(memory_space=pltpu.HBM)


def call(body, outs, ins, scratch=(), megabytes=8, where=VMEM, aliases=()):
    return pl.pallas_call(
        body,
        out_shape=outs,
        in_specs=ins,
        out_specs=where if isinstance(where, tuple) else jax.tree.map(lambda _: where, outs),
        input_output_aliases=dict(aliases),
        scratch_shapes=scratch,
        compiler_params=pltpu.CompilerParams(vmem_limit_bytes=megabytes << 20),
    )


def places(capacity, groups, owner, local):
    seeds, neighbours = owner.shape
    lane = iota((seeds, groups), 1)
    named = jnp.zeros((seeds, groups), f32)
    wanted = jnp.zeros((seeds, groups), i32)
    for k in range(neighbours):
        hit = owner[:, k : k + 1] == lane
        named = jnp.where(hit, 1.0, named)
        wanted = jnp.where(hit, local[:, k : k + 1], wanted)
    before = (iota((seeds, seeds), 1) < iota((seeds, seeds), 0)).astype(f32)
    earlier = dot(before.astype(bf16), named.astype(bf16)).astype(i32)
    return named > 0, earlier, wanted


def request_body(
    capacity,
    core_ref,
    owner_hbm,
    local_hbm,
    weight_hbm,
    labels_hbm,
    pairs_hbm,
    table_ref,
    codes_ref,
    weights_ref,
    label_ref,
    pairs_ref,
    owner_ref,
    local_ref,
    weight_ref,
    labels_ref,
    arrivals,
):
    del core_ref
    small = zip((owner_hbm, local_hbm, weight_hbm, labels_hbm), (owner_ref, local_ref, weight_ref, labels_ref))
    copies = [pltpu.make_async_copy(source, target, arrivals.at[i]) for i, (source, target) in enumerate(small)]
    for copy in copies:
        copy.start()
    pairs = pltpu.make_async_copy(pairs_hbm, pairs_ref, arrivals.at[len(copies)])
    pairs.start()
    for copy in copies:
        copy.wait()
    groups = table_ref.shape[0]
    owner = owner_ref[...]
    seeds, neighbours = owner.shape
    named, earlier, wanted = places(capacity, groups, owner, local_ref[...])
    place = jnp.where(named, earlier, -1)
    slot = iota((capacity, groups), 0)
    table = jnp.zeros((capacity, groups), i32)
    for s in range(seeds):
        table = jnp.where(place[s : s + 1, :] == slot, wanted[s : s + 1, :], table)
    spare = jnp.zeros((LANES - capacity, groups), i32)
    table_ref[...] = jnp.concatenate([table, spare], axis=0).T
    code_of = coded_slots(iota((seeds, groups), 1) * capacity + earlier)
    owner_t = owner.T
    weight_t = weight_ref[...].T
    lane = iota((neighbours, groups), 1)
    own = []
    for s in range(seeds):
        own.append(jnp.where(owner_t[:, s : s + 1] == lane, code_of[s : s + 1, :], 0.0).astype(bf16))
        rows = pl.ds(s * neighbours, neighbours)
        weights_ref[rows, :] = jnp.broadcast_to(weight_t[:, s : s + 1], (neighbours, weights_ref.shape[1]))
    everything = jnp.ones((groups, codes_ref.shape[1]), bf16)
    codes_ref[...] = dot(jnp.concatenate(own, axis=0), everything).astype(bf16)
    diagonal = iota((seeds, seeds), 0) == iota((seeds, seeds), 1)
    label = jnp.sum(jnp.where(diagonal, labels_ref[...].astype(f32), 0.0), axis=1, keepdims=True)
    label_ref[...] = label.astype(i32)
    pairs.wait()


def coded_slots(slot):
    return ((128 + (slot & 127)) * (1 << (slot >> 7))).astype(f32)


def serve_body(
    capacity,
    asked_ref,
    pairs_ref,
    first_hbm,
    second_hbm,
    third_t_hbm,
    rows_ref,
    first_ref,
    second_ref,
    third_t_ref,
    stage_ref,
    wide_ref,
    turned_ref,
    index_ref,
    arrival,
    params,
):
    layers = zip((first_hbm, second_hbm, third_t_hbm), (first_ref, second_ref, third_t_ref))
    copies = [pltpu.make_async_copy(source, target, params.at[i]) for i, (source, target) in enumerate(layers)]
    asked = asked_ref[...]
    turned_ref[...] = asked.T[:capacity, :] >> 1
    index = pltpu.make_async_copy(turned_ref, index_ref, arrival)
    index.start()
    for copy in copies:
        copy.start()
    index.wait()
    odd = (asked & 1) > 0
    groups = wide_ref.shape[0]
    size = asked.shape[0] // groups
    for group in range(groups):
        span = slice(group * size, (group + 1) * size)
        for p in range(capacity):
            stage = stage_ref.at[p % stage_ref.shape[0]]
            for source in range(size):
                stage[2 * source : 2 * source + 2, :] = pairs_ref[index_ref[p, span.start + source]].astype(f32)
            first = stage[pl.ds(0, size, stride=2), :]
            second = stage[pl.ds(1, size, stride=2), :]
            wide_ref[group, pl.ds(p, size, stride=capacity), :] = jnp.where(odd[span, p : p + 1], second, first)
        rows_ref[span] = wide_ref[group, : size * capacity, :].reshape(size, capacity, -1).astype(bf16)
    for copy in copies:
        copy.wait()


def step_body(
    total_seeds,
    blocks,
    core_ref,
    codes_ref,
    arrived_ref,
    weights_ref,
    label_ref,
    first_ref,
    second_ref,
    third_t_ref,
    logits_hbm,
    send_ref,
    terms_ref,
    x_ref,
    first_act_ref,
    weighted_ref,
    second_act_ref,
    second_grad_ref,
    first_grad_ref,
    grads_ref,
    logits_ref,
    leaving,
):
    seeds, classes = logits_ref.shape
    rows = codes_ref.shape[0]
    neighbours = rows // seeds
    zero = jnp.zeros((), bf16)
    own_rows = [slice(b * rows // blocks, (b + 1) * rows // blocks) for b in range(blocks)]
    own_seeds = [slice(b * seeds // blocks, (b + 1) * seeds // blocks) for b in range(blocks)]
    size, seed_size = rows // blocks, seeds // blocks

    def rectified(pre):
        return jnp.maximum(pre.astype(bf16), zero)

    def masked(act, grad):
        return jnp.where(act > zero, grad.astype(bf16), zero)

    def halves(ref, parts):
        wide = ref.shape[2]
        for part, r in zip(parts, own_rows):
            for h in range(2):
                ref[h, r, :] = part[:, h * wide : (h + 1) * wide]

    slots = arrived_ref.shape[0]
    side = slots // 2
    arrived = jnp.concatenate([arrived_ref[:side, :], arrived_ref[side:, :]], axis=1)
    every_code = coded_slots(iota((16, side), 1)).astype(bf16)
    every_code = jnp.concatenate([every_code] * (size // 16), axis=0)
    bound = float(128 << (side >> 7))
    x = []
    for r in own_rows:
        late = codes_ref[r, :] >= jnp.asarray(bound, bf16)
        code = jnp.where(late, codes_ref[r, :] * jnp.asarray(128.0 / bound, bf16), codes_ref[r, :])
        code = jnp.concatenate([code] * (side // LANES), axis=1)
        pick = jnp.where(code == every_code, jnp.ones((), bf16), zero)
        both = dot(pick, arrived).astype(bf16)
        x.append(jnp.where(late, both[:, LANES:], both[:, :LANES]))
        x_ref[r, :] = x[-1]
    first_act = [rectified(dot(part, first_ref[...])) for part in x]
    second_act = [rectified(dot(part, second_ref[...])) for part in first_act]
    for part, r in zip(first_act, own_rows):
        first_act_ref[r, :] = part
    halves(second_act_ref, second_act)
    weighted, terms = [], []
    for act, r, s in zip(second_act, own_rows, own_seeds):
        row_logits = dot(act, third_t_ref[...], ((1,), (1,)))
        weight = weights_ref[r, :]
        weight = jnp.concatenate([weight, weight[:, : classes - LANES]], axis=1)
        logits = jnp.sum((weight * row_logits).reshape(seed_size, neighbours, classes), axis=1)
        logits_ref[s, :] = logits
        highest = jnp.max(logits, axis=1, keepdims=True)
        log_total = jnp.log(jnp.sum(jnp.exp(logits - highest), axis=1, keepdims=True)) + highest
        onehot = jnp.where(label_ref[s, :] == iota((seed_size, classes), 1), 1.0, 0.0)
        terms.append(log_total - jnp.sum(onehot * logits, axis=1, keepdims=True))
        logit_grad = (jnp.exp(logits - log_total) - onehot) / total_seeds
        every = jnp.broadcast_to(logit_grad[:, None, :], (seed_size, neighbours, classes)).reshape(size, classes)
        weighted.append((weight * every).astype(bf16))
        weighted_ref[r, :] = weighted[-1]
    logits_copy = pltpu.make_async_copy(logits_ref, logits_hbm, leaving)
    logits_copy.start()
    second_grad = [masked(a, dot(g, third_t_ref[...])) for a, g in zip(second_act, weighted)]
    halves(second_grad_ref, second_grad)
    first_grad = [masked(a, dot(g, second_ref[...], ((1,), (1,)))) for a, g in zip(first_act, second_grad)]
    halves(first_grad_ref, first_grad)
    diagonal = iota((seeds, LANES), 0) == iota((seeds, LANES), 1)
    loss_row = jnp.sum(jnp.where(diagonal, jnp.concatenate(terms, axis=0), 0.0), axis=0, keepdims=True)
    loss_row = loss_row.astype(bf16).astype(f32)
    terms_ref[...] = jnp.broadcast_to(loss_row, terms_ref.shape)
    other = 1 - core_ref[0]
    write_half(
        grads_ref, loss_row, x_ref, first_act_ref, weighted_ref, second_act_ref, second_grad_ref, first_grad_ref, other
    )
    send_ref[...] = grads_ref[...].astype(bf16)
    logits_copy.wait()


def write_half(out_ref, loss_row, x_ref, first_act_ref, weighted_ref, second_act_ref, second_grad_ref, first_grad_ref, half):
    down = ((0,), (0,))
    first = dot(x_ref[...], first_grad_ref[half], down)
    second = dot(first_act_ref[...], second_grad_ref[half], down)
    third = dot(weighted_ref[...], second_act_ref[half], down)
    parts = first.shape[1] // LANES
    tall = out_ref.shape[0] // parts
    for j in range(parts):
        at = j * tall
        for piece in (first, second, third):
            out_ref[at : at + piece.shape[0], :] = piece[:, j * LANES : (j + 1) * LANES]
            at += piece.shape[0]
        out_ref[at : (j + 1) * tall, :] = jnp.zeros(((j + 1) * tall - at, LANES), f32)
        out_ref[at : at + 1, :] = loss_row


def keep_body(
    core_ref, terms_ref, x_ref, first_act_ref, weighted_ref, second_act_ref, second_grad_ref, first_grad_ref, keep_ref
):
    write_half(
        keep_ref,
        terms_ref[:1, :],
        x_ref,
        first_act_ref,
        weighted_ref,
        second_act_ref,
        second_grad_ref,
        first_grad_ref,
        core_ref[0],
    )


def total_body(chips, parts_ref, total_ref):
    rows = parts_ref.shape[0]
    chunk = rows // chips
    tall = -(-chunk // 8) * 8
    column = iota((tall, rows), 1)
    which = ((column.astype(f32) + 0.5) / chunk).astype(i32)
    same = jnp.where(column - which * chunk == iota((tall, rows), 0), 1.0, 0.0).astype(bf16)
    total = dot(same, parts_ref[...]).astype(bf16)
    total_ref[...] = dot(same, total, ((0,), (0,))).astype(bf16)


def columns(half, half_ref, outs, stages, arrivals):
    copies = []
    at = 0
    for i, (out, stage) in enumerate(zip(outs, stages)):
        size, wide = stage.shape
        parts = wide // LANES
        tall = half_ref.shape[0] // parts
        for j in range(parts):
            stage[:, j * LANES : (j + 1) * LANES] = half_ref[j * tall + at : j * tall + at + size, :].astype(f32)
        span = pl.ds(pl.multiple_of(half * wide, wide), wide)
        copies.append(pltpu.make_async_copy(stage, out.at[:, span], arrivals.at[i]))
        copies[-1].start()
        at += size
    for copy in copies:
        copy.wait()


def own_body(total_seeds, core_ref, own_ref, first_hbm, second_hbm, third_t_hbm, loss_ref, *scratch):
    outs = (first_hbm, second_hbm, third_t_hbm)
    at = sum(out.shape[0] for out in outs)
    loss_ref[...] = jnp.sum(own_ref[at : at + 1, :].astype(f32), axis=1, keepdims=True) / total_seeds
    columns(core_ref[0], own_ref, outs, scratch[:3], scratch[3])


def other_body(core_ref, other_ref, given_first, given_second, given_third_t, first_hbm, second_hbm, third_t_hbm, *scratch):
    del given_first, given_second, given_third_t
    columns(1 - core_ref[0], other_ref, (first_hbm, second_hbm, third_t_hbm), scratch[:3], scratch[3])


def everywhere(parts, axis):
    return lax.all_to_all(parts, axis, 0, 0, tiled=True)


def on_device(features, nbr_owner, nbr_local, ppr_weight, labels, w_first, w_second, w_third):
    groups = lax.axis_size(NODES)
    chips = lax.axis_size(CHIPS)
    seeds, neighbours = nbr_owner.shape
    capacity = min(seeds, 2 * seeds * neighbours // groups)
    width, hidden = w_first.shape
    classes = w_third.shape[1]
    total_seeds = float(seeds * groups)
    slots = groups * capacity
    shape = jax.ShapeDtypeStruct
    core = lax.axis_index(CORE).astype(i32).reshape(1)
    swap = [(0, 1), (1, 0)]

    pairs = features.reshape(-1, 2, width)
    rows = seeds * neighbours
    table, codes, weights, label, pairs = call(
        functools.partial(request_body, capacity),
        (
            shape((groups, LANES), i32),
            shape((rows, LANES), bf16),
            shape((rows, LANES), f32),
            shape((seeds, 1), i32),
            pltpu.VMEM(pairs.shape, bf16),
        ),
        [SMEM] + [FAR] * 5,
        [
            *(pltpu.VMEM((seeds, neighbours), t) for t in (i32, i32, f32)),
            pltpu.VMEM((1, seeds), i32),
            pltpu.SemaphoreType.DMA((5,)),
        ],
    )(
        core,
        *(
            pltpu.with_memory_space_constraint(a, pltpu.HBM)
            for a in (nbr_owner, nbr_local, ppr_weight, labels.reshape(1, -1), pairs)
        ),
    )
    asked = everywhere(table.reshape(groups, 1, LANES), NODES).reshape(groups, LANES)
    params = (w_first, w_second, w_third.T)
    served, *params = call(
        functools.partial(serve_body, capacity),
        (shape((groups, capacity, width), bf16), *(pltpu.VMEM(p.shape, bf16) for p in params)),
        [VMEM, VMEM, FAR, FAR, FAR],
        [
            pltpu.VMEM((4, groups // 2 + 8, width), f32),
            pltpu.VMEM((4, (groups // 4 + 1) * capacity, width), f32),
            pltpu.VMEM((capacity, groups), i32),
            pltpu.SMEM((capacity, groups), i32),
            pltpu.SemaphoreType.DMA,
            pltpu.SemaphoreType.DMA((3,)),
        ],
        16,
    )(asked, pairs, *(pltpu.with_memory_space_constraint(p, pltpu.HBM) for p in params))
    arrived = everywhere(served, NODES).reshape(slots, width)

    half = hidden // 2
    blocks = half // LANES
    tall = 2 * chips // blocks * -(-(width + hidden + classes + 1) * blocks // (2 * chips))
    grads = (blocks * tall, LANES)
    seed_logits, send, *kept = call(
        functools.partial(step_body, total_seeds, 2),
        (
            pltpu.HBM((seeds, classes), f32),
            shape(grads, bf16),
            shape((8, LANES), f32),
            shape((rows, width), bf16),
            shape((rows, hidden), bf16),
            shape((rows, classes), bf16),
            *(shape((2, rows, half), bf16) for _ in range(3)),
        ),
        [SMEM] + [VMEM] * 7,
        [pltpu.VMEM(grads, f32), pltpu.VMEM((seeds, classes), f32), pltpu.SemaphoreType.DMA],
        32,
        (FAR, *[VMEM] * 8),
    )(core, codes, arrived, weights, label, *params)
    near = lax.ppermute(send, CORE, swap)
    keep = call(keep_body, shape(grads, f32), [SMEM] + [VMEM] * 7, (), 16)(core, *kept)
    parts = (keep + near.astype(f32)).astype(bf16)
    mine = everywhere(parts.reshape(-1, 2, LANES), CHIPS).reshape(grads)
    totals = call(functools.partial(total_body, chips), shape(grads, bf16), [VMEM])(mine)
    own = everywhere(totals.reshape(-1, 2, LANES), CHIPS).reshape(grads)
    other = lax.ppermute(own, CORE, swap)
    sizes = (width, hidden, classes)
    scratch = [*(pltpu.VMEM((n, half), f32) for n in sizes), pltpu.SemaphoreType.DMA((3,))]
    sums = tuple(pltpu.HBM((n, hidden), f32) for n in sizes)
    *started, loss = call(
        functools.partial(own_body, total_seeds),
        (*sums, shape((1, 1), f32)),
        [SMEM, VMEM],
        scratch,
        8,
        (FAR, FAR, FAR, VMEM),
    )(core, own)
    grad_first, grad_second, grad_third_t = call(
        other_body, sums, [SMEM, VMEM, FAR, FAR, FAR], scratch, 8, FAR, {2: 0, 3: 1, 4: 2}
    )(core, other, *started)
    return (loss.reshape(()), seed_logits, grad_first, grad_second, grad_third_t.T)


def solution(mesh):
    finer = Mesh(mesh.devices.reshape(4, 4, 4, 2), NODES)
    placed = (
        P(NODES, None),
        P(NODES, None),
        P(NODES, None),
        P(NODES, None),
        P(NODES),
        P(),
        P(),
        P(),
    )
    return jax.shard_map(
        on_device,
        mesh=finer,
        in_specs=placed,
        out_specs=(P(), P(NODES, None), P(), P(), P()),
        check_vma=False,
    )
```

```python
import functools

import jax
import jax.numpy as jnp
from jax import lax
from jax.experimental import pallas as pl
from jax.experimental.pallas import tpu as pltpu
from jax.sharding import Mesh
from jax.sharding import PartitionSpec as P

CHIPS = ("nodes_0", "nodes_1", "nodes_2")
CORE = "nodes_3"
NODES = (*CHIPS, CORE)
LANES = 128

bf16 = jnp.bfloat16
f32 = jnp.float32
i32 = jnp.int32


def iota(shape, dim):
    return lax.broadcasted_iota(i32, shape, dim)


def dot(a, b, over=((1,), (0,))):
    return lax.dot_general(a, b, (over, ((), ())), preferred_element_type=f32)


VMEM = pl.BlockSpec(memory_space=pltpu.VMEM)
SMEM = pl.BlockSpec(memory_space=pltpu.SMEM)
FAR = pl.BlockSpec(memory_space=pltpu.HBM)


def call(body, outs, ins, scratch=(), megabytes=8, where=VMEM, aliases=()):
    return pl.pallas_call(
        body,
        out_shape=outs,
        in_specs=ins,
        out_specs=where if isinstance(where, tuple) else jax.tree.map(lambda _: where, outs),
        input_output_aliases=dict(aliases),
        scratch_shapes=scratch,
        compiler_params=pltpu.CompilerParams(vmem_limit_bytes=megabytes << 20),
    )


def places(capacity, groups, owner, local):
    seeds, neighbours = owner.shape
    lane = iota((seeds, groups), 1)
    named = jnp.zeros((seeds, groups), f32)
    wanted = jnp.zeros((seeds, groups), i32)
    for k in range(neighbours):
        hit = owner[:, k : k + 1] == lane
        named = jnp.where(hit, 1.0, named)
        wanted = jnp.where(hit, local[:, k : k + 1], wanted)
    before = (iota((seeds, seeds), 1) < iota((seeds, seeds), 0)).astype(f32)
    earlier = dot(before.astype(bf16), named.astype(bf16)).astype(i32)
    return named > 0, earlier, wanted


def request_body(
    capacity,
    core_ref,
    owner_hbm,
    local_hbm,
    weight_hbm,
    labels_hbm,
    pairs_hbm,
    table_ref,
    codes_ref,
    weights_ref,
    label_ref,
    pairs_ref,
    owner_ref,
    local_ref,
    weight_ref,
    labels_ref,
    arrivals,
):
    del core_ref
    small = zip((owner_hbm, local_hbm, weight_hbm, labels_hbm), (owner_ref, local_ref, weight_ref, labels_ref))
    copies = [pltpu.make_async_copy(source, target, arrivals.at[i]) for i, (source, target) in enumerate(small)]
    for copy in copies:
        copy.start()
    pairs = pltpu.make_async_copy(pairs_hbm, pairs_ref, arrivals.at[len(copies)])
    pairs.start()
    for copy in copies:
        copy.wait()
    groups = table_ref.shape[0]
    owner = owner_ref[...]
    seeds, neighbours = owner.shape
    named, earlier, wanted = places(capacity, groups, owner, local_ref[...])
    place = jnp.where(named, earlier, -1)
    slot = iota((capacity, groups), 0)
    table = jnp.zeros((capacity, groups), i32)
    for s in range(seeds):
        table = jnp.where(place[s : s + 1, :] == slot, wanted[s : s + 1, :], table)
    spare = jnp.zeros((LANES - capacity, groups), i32)
    table_ref[...] = jnp.concatenate([table, spare], axis=0).T
    code_of = coded_slots(iota((seeds, groups), 1) * capacity + earlier)
    owner_t = owner.T
    weight_t = weight_ref[...].T
    lane = iota((neighbours, groups), 1)
    own = []
    for s in range(seeds):
        own.append(jnp.where(owner_t[:, s : s + 1] == lane, code_of[s : s + 1, :], 0.0).astype(bf16))
        rows = pl.ds(s * neighbours, neighbours)
        weights_ref[rows, :] = jnp.broadcast_to(weight_t[:, s : s + 1], (neighbours, weights_ref.shape[1]))
    everything = jnp.ones((groups, codes_ref.shape[1]), bf16)
    codes_ref[...] = dot(jnp.concatenate(own, axis=0), everything).astype(bf16)
    diagonal = iota((seeds, seeds), 0) == iota((seeds, seeds), 1)
    label = jnp.sum(jnp.where(diagonal, labels_ref[...].astype(f32), 0.0), axis=1, keepdims=True)
    label_ref[...] = label.astype(i32)
    pairs.wait()


def coded_slots(slot):
    return ((128 + (slot & 127)) * (1 << (slot >> 7))).astype(f32)


def serve_body(
    capacity,
    asked_ref,
    pairs_ref,
    first_hbm,
    second_hbm,
    third_t_hbm,
    rows_ref,
    first_ref,
    second_ref,
    third_t_ref,
    stage_ref,
    wide_ref,
    turned_ref,
    index_ref,
    arrival,
    params,
):
    layers = zip((first_hbm, second_hbm, third_t_hbm), (first_ref, second_ref, third_t_ref))
    copies = [pltpu.make_async_copy(source, target, params.at[i]) for i, (source, target) in enumerate(layers)]
    asked = asked_ref[...]
    turned_ref[...] = asked.T[:capacity, :] >> 1
    index = pltpu.make_async_copy(turned_ref, index_ref, arrival)
    index.start()
    for copy in copies:
        copy.start()
    index.wait()
    odd = (asked & 1) > 0
    groups = wide_ref.shape[0]
    size = asked.shape[0] // groups
    for group in range(groups):
        span = slice(group * size, (group + 1) * size)
        for p in range(capacity):
            stage = stage_ref.at[p % stage_ref.shape[0]]
            for source in range(size):
                stage[2 * source : 2 * source + 2, :] = pairs_ref[index_ref[p, span.start + source]].astype(f32)
            first = stage[pl.ds(0, size, stride=2), :]
            second = stage[pl.ds(1, size, stride=2), :]
            wide_ref[group, pl.ds(p, size, stride=capacity), :] = jnp.where(odd[span, p : p + 1], second, first)
        rows_ref[span] = wide_ref[group, : size * capacity, :].reshape(size, capacity, -1).astype(bf16)
    for copy in copies:
        copy.wait()


def step_body(
    total_seeds,
    blocks,
    core_ref,
    codes_ref,
    arrived_ref,
    weights_ref,
    label_ref,
    first_ref,
    second_ref,
    third_t_ref,
    logits_hbm,
    send_ref,
    terms_ref,
    x_ref,
    first_act_ref,
    weighted_ref,
    second_act_ref,
    second_grad_ref,
    first_grad_ref,
    grads_ref,
    logits_ref,
    leaving,
):
    seeds, classes = logits_ref.shape
    rows = codes_ref.shape[0]
    neighbours = rows // seeds
    zero = jnp.zeros((), bf16)
    own_rows = [slice(b * rows // blocks, (b + 1) * rows // blocks) for b in range(blocks)]
    own_seeds = [slice(b * seeds // blocks, (b + 1) * seeds // blocks) for b in range(blocks)]
    size, seed_size = rows // blocks, seeds // blocks

    def rectified(pre):
        return jnp.maximum(pre.astype(bf16), zero)

    def masked(act, grad):
        return jnp.where(act > zero, grad.astype(bf16), zero)

    def halves(ref, parts):
        wide = ref.shape[2]
        for part, r in zip(parts, own_rows):
            for h in range(2):
                ref[h, r, :] = part[:, h * wide : (h + 1) * wide]

    slots = arrived_ref.shape[0]
    side = slots // 2
    arrived = jnp.concatenate([arrived_ref[:side, :], arrived_ref[side:, :]], axis=1)
    every_code = coded_slots(iota((16, side), 1)).astype(bf16)
    every_code = jnp.concatenate([every_code] * (size // 16), axis=0)
    bound = float(128 << (side >> 7))
    x = []
    for r in own_rows:
        late = codes_ref[r, :] >= jnp.asarray(bound, bf16)
        code = jnp.where(late, codes_ref[r, :] * jnp.asarray(128.0 / bound, bf16), codes_ref[r, :])
        code = jnp.concatenate([code] * (side // LANES), axis=1)
        pick = jnp.where(code == every_code, jnp.ones((), bf16), zero)
        both = dot(pick, arrived).astype(bf16)
        x.append(jnp.where(late, both[:, LANES:], both[:, :LANES]))
        x_ref[r, :] = x[-1]
    first_act = [rectified(dot(part, first_ref[...])) for part in x]
    second_act = [rectified(dot(part, second_ref[...])) for part in first_act]
    for part, r in zip(first_act, own_rows):
        first_act_ref[r, :] = part
    halves(second_act_ref, second_act)
    weighted, terms = [], []
    for act, r, s in zip(second_act, own_rows, own_seeds):
        row_logits = dot(act, third_t_ref[...], ((1,), (1,)))
        weight = weights_ref[r, :]
        weight = jnp.concatenate([weight, weight[:, : classes - LANES]], axis=1)
        logits = jnp.sum((weight * row_logits).reshape(seed_size, neighbours, classes), axis=1)
        logits_ref[s, :] = logits
        highest = jnp.max(logits, axis=1, keepdims=True)
        log_total = jnp.log(jnp.sum(jnp.exp(logits - highest), axis=1, keepdims=True)) + highest
        onehot = jnp.where(label_ref[s, :] == iota((seed_size, classes), 1), 1.0, 0.0)
        terms.append(log_total - jnp.sum(onehot * logits, axis=1, keepdims=True))
        logit_grad = (jnp.exp(logits - log_total) - onehot) / total_seeds
        every = jnp.broadcast_to(logit_grad[:, None, :], (seed_size, neighbours, classes)).reshape(size, classes)
        weighted.append((weight * every).astype(bf16))
        weighted_ref[r, :] = weighted[-1]
    logits_copy = pltpu.make_async_copy(logits_ref, logits_hbm, leaving)
    logits_copy.start()
    second_grad = [masked(a, dot(g, third_t_ref[...])) for a, g in zip(second_act, weighted)]
    halves(second_grad_ref, second_grad)
    first_grad = [masked(a, dot(g, second_ref[...], ((1,), (1,)))) for a, g in zip(first_act, second_grad)]
    halves(first_grad_ref, first_grad)
    diagonal = iota((seeds, LANES), 0) == iota((seeds, LANES), 1)
    loss_row = jnp.sum(jnp.where(diagonal, jnp.concatenate(terms, axis=0), 0.0), axis=0, keepdims=True)
    loss_row = loss_row.astype(bf16).astype(f32)
    terms_ref[...] = jnp.broadcast_to(loss_row, terms_ref.shape)
    other = 1 - core_ref[0]
    write_half(
        grads_ref, loss_row, x_ref, first_act_ref, weighted_ref, second_act_ref, second_grad_ref, first_grad_ref, other
    )
    send_ref[...] = grads_ref[...].astype(bf16)
    logits_copy.wait()


def write_half(out_ref, loss_row, x_ref, first_act_ref, weighted_ref, second_act_ref, second_grad_ref, first_grad_ref, half):
    down = ((0,), (0,))
    first = dot(x_ref[...], first_grad_ref[half], down)
    second = dot(first_act_ref[...], second_grad_ref[half], down)
    third = dot(weighted_ref[...], second_act_ref[half], down)
    parts = first.shape[1] // LANES
    tall = out_ref.shape[0] // parts
    for j in range(parts):
        at = j * tall
        for piece in (first, second, third):
            out_ref[at : at + piece.shape[0], :] = piece[:, j * LANES : (j + 1) * LANES]
            at += piece.shape[0]
        out_ref[at : (j + 1) * tall, :] = jnp.zeros(((j + 1) * tall - at, LANES), f32)
        out_ref[at : at + 1, :] = loss_row


def keep_body(
    core_ref, terms_ref, x_ref, first_act_ref, weighted_ref, second_act_ref, second_grad_ref, first_grad_ref, keep_ref
):
    write_half(
        keep_ref,
        terms_ref[:1, :],
        x_ref,
        first_act_ref,
        weighted_ref,
        second_act_ref,
        second_grad_ref,
        first_grad_ref,
        core_ref[0],
    )


def total_body(chips, parts_ref, total_ref):
    rows = parts_ref.shape[0]
    chunk = rows // chips
    tall = -(-chunk // 8) * 8
    column = iota((tall, rows), 1)
    which = ((column.astype(f32) + 0.5) / chunk).astype(i32)
    same = jnp.where(column - which * chunk == iota((tall, rows), 0), 1.0, 0.0).astype(bf16)
    total = dot(same, parts_ref[...]).astype(bf16)
    total_ref[...] = dot(same, total, ((0,), (0,))).astype(bf16)


def columns(half, half_ref, outs, stages, arrivals):
    copies = []
    at = 0
    for i, (out, stage) in enumerate(zip(outs, stages)):
        size, wide = stage.shape
        parts = wide // LANES
        tall = half_ref.shape[0] // parts
        for j in range(parts):
            stage[:, j * LANES : (j + 1) * LANES] = half_ref[j * tall + at : j * tall + at + size, :].astype(f32)
        span = pl.ds(pl.multiple_of(half * wide, wide), wide)
        copies.append(pltpu.make_async_copy(stage, out.at[:, span], arrivals.at[i]))
        copies[-1].start()
        at += size
    for copy in copies:
        copy.wait()


def own_body(total_seeds, core_ref, own_ref, first_hbm, second_hbm, third_t_hbm, loss_hbm, loss_ref, leaving, *scratch):
    outs = (first_hbm, second_hbm, third_t_hbm)
    at = sum(out.shape[0] for out in outs)
    loss_ref[...] = jnp.sum(own_ref[at : at + 1, :].astype(f32), axis=1, keepdims=True) / total_seeds
    copy = pltpu.make_async_copy(loss_ref, loss_hbm, leaving)
    copy.start()
    columns(core_ref[0], own_ref, outs, scratch[:3], scratch[3])
    copy.wait()


def other_body(core_ref, other_ref, given_first, given_second, given_third_t, first_hbm, second_hbm, third_t_hbm, *scratch):
    del given_first, given_second, given_third_t
    columns(1 - core_ref[0], other_ref, (first_hbm, second_hbm, third_t_hbm), scratch[:3], scratch[3])


def everywhere(parts, axis):
    return lax.all_to_all(parts, axis, 0, 0, tiled=True)


def on_device(features, nbr_owner, nbr_local, ppr_weight, labels, w_first, w_second, w_third):
    groups = lax.axis_size(NODES)
    chips = lax.axis_size(CHIPS)
    seeds, neighbours = nbr_owner.shape
    capacity = min(seeds, 2 * seeds * neighbours // groups)
    width, hidden = w_first.shape
    classes = w_third.shape[1]
    total_seeds = float(seeds * groups)
    slots = groups * capacity
    shape = jax.ShapeDtypeStruct
    core = lax.axis_index(CORE).astype(i32).reshape(1)
    swap = [(0, 1), (1, 0)]

    pairs = features.reshape(-1, 2, width)
    rows = seeds * neighbours
    table, codes, weights, label, pairs = call(
        functools.partial(request_body, capacity),
        (
            shape((groups, LANES), i32),
            shape((rows, LANES), bf16),
            shape((rows, LANES), f32),
            shape((seeds, 1), i32),
            pltpu.VMEM(pairs.shape, bf16),
        ),
        [SMEM] + [FAR] * 5,
        [
            *(pltpu.VMEM((seeds, neighbours), t) for t in (i32, i32, f32)),
            pltpu.VMEM((1, seeds), i32),
            pltpu.SemaphoreType.DMA((5,)),
        ],
    )(
        core,
        *(
            pltpu.with_memory_space_constraint(a, pltpu.HBM)
            for a in (nbr_owner, nbr_local, ppr_weight, labels.reshape(1, -1), pairs)
        ),
    )
    asked = everywhere(table.reshape(groups, 1, LANES), NODES).reshape(groups, LANES)
    params = (w_first, w_second, w_third.T)
    served, *params = call(
        functools.partial(serve_body, capacity),
        (shape((groups, capacity, width), bf16), *(pltpu.VMEM(p.shape, bf16) for p in params)),
        [VMEM, VMEM, FAR, FAR, FAR],
        [
            pltpu.VMEM((4, groups // 2 + 8, width), f32),
            pltpu.VMEM((4, (groups // 4 + 1) * capacity, width), f32),
            pltpu.VMEM((capacity, groups), i32),
            pltpu.SMEM((capacity, groups), i32),
            pltpu.SemaphoreType.DMA,
            pltpu.SemaphoreType.DMA((3,)),
        ],
        16,
    )(asked, pairs, *(pltpu.with_memory_space_constraint(p, pltpu.HBM) for p in params))
    arrived = everywhere(served, NODES).reshape(slots, width)

    half = hidden // 2
    blocks = half // LANES
    tall = 2 * chips // blocks * -(-(width + hidden + classes + 1) * blocks // (2 * chips))
    grads = (blocks * tall, LANES)
    seed_logits, send, *kept = call(
        functools.partial(step_body, total_seeds, 2),
        (
            pltpu.HBM((seeds, classes), f32),
            shape(grads, bf16),
            shape((8, LANES), f32),
            shape((rows, width), bf16),
            shape((rows, hidden), bf16),
            shape((rows, classes), bf16),
            *(shape((2, rows, half), bf16) for _ in range(3)),
        ),
        [SMEM] + [VMEM] * 7,
        [pltpu.VMEM(grads, f32), pltpu.VMEM((seeds, classes), f32), pltpu.SemaphoreType.DMA],
        32,
        (FAR, *[VMEM] * 8),
    )(core, codes, arrived, weights, label, *params)
    near = lax.ppermute(send, CORE, swap)
    keep = call(keep_body, shape(grads, f32), [SMEM] + [VMEM] * 7, (), 16)(core, *kept)
    parts = (keep + near.astype(f32)).astype(bf16)
    mine = everywhere(parts.reshape(-1, 2, LANES), CHIPS).reshape(grads)
    totals = call(functools.partial(total_body, chips), shape(grads, bf16), [VMEM])(mine)
    own = everywhere(totals.reshape(-1, 2, LANES), CHIPS).reshape(grads)
    other = lax.ppermute(own, CORE, swap)
    sizes = (width, hidden, classes)
    scratch = [*(pltpu.VMEM((n, half), f32) for n in sizes), pltpu.SemaphoreType.DMA((3,))]
    sums = tuple(pltpu.HBM((n, hidden), f32) for n in sizes)
    *started, loss = call(
        functools.partial(own_body, total_seeds),
        (*sums, pltpu.HBM((1, 1), f32)),
        [SMEM, VMEM],
        [pltpu.VMEM((1, 1), f32), pltpu.SemaphoreType.DMA, *scratch],
        8,
        FAR,
    )(core, own)
    grad_first, grad_second, grad_third_t = call(
        other_body, sums, [SMEM, VMEM, FAR, FAR, FAR], scratch, 8, FAR, {2: 0, 3: 1, 4: 2}
    )(core, other, *started)
    return (loss.reshape(()), seed_logits, grad_first, grad_second, grad_third_t.T)


def solution(mesh):
    finer = Mesh(mesh.devices.reshape(4, 4, 4, 2), NODES)
    placed = (
        P(NODES, None),
        P(NODES, None),
        P(NODES, None),
        P(NODES, None),
        P(NODES),
        P(),
        P(),
        P(),
    )
    return jax.shard_map(
        on_device,
        mesh=finer,
        in_specs=placed,
        out_specs=(P(), P(NODES, None), P(), P(), P()),
        check_vma=False,
    )
```

```python
import functools

import jax
import jax.numpy as jnp
from jax import lax
from jax.experimental import pallas as pl
from jax.experimental.pallas import tpu as pltpu
from jax.sharding import Mesh
from jax.sharding import PartitionSpec as P

CHIPS = ("nodes_0", "nodes_1", "nodes_2")
CORE = "nodes_3"
NODES = (*CHIPS, CORE)
LANES = 128

bf16 = jnp.bfloat16
f32 = jnp.float32
i32 = jnp.int32


def iota(shape, dim):
    return lax.broadcasted_iota(i32, shape, dim)


def dot(a, b, over=((1,), (0,))):
    return lax.dot_general(a, b, (over, ((), ())), preferred_element_type=f32)


VMEM = pl.BlockSpec(memory_space=pltpu.VMEM)
SMEM = pl.BlockSpec(memory_space=pltpu.SMEM)
FAR = pl.BlockSpec(memory_space=pltpu.HBM)


def call(body, outs, ins, scratch=(), megabytes=8, where=VMEM, aliases=()):
    return pl.pallas_call(
        body,
        out_shape=outs,
        in_specs=ins,
        out_specs=where if isinstance(where, tuple) else jax.tree.map(lambda _: where, outs),
        input_output_aliases=dict(aliases),
        scratch_shapes=scratch,
        compiler_params=pltpu.CompilerParams(vmem_limit_bytes=megabytes << 20),
    )


def places(capacity, groups, owner, local):
    seeds, neighbours = owner.shape
    lane = iota((seeds, groups), 1)
    named = jnp.zeros((seeds, groups), f32)
    wanted = jnp.zeros((seeds, groups), i32)
    for k in range(neighbours):
        hit = owner[:, k : k + 1] == lane
        named = jnp.where(hit, 1.0, named)
        wanted = jnp.where(hit, local[:, k : k + 1], wanted)
    before = (iota((seeds, seeds), 1) < iota((seeds, seeds), 0)).astype(f32)
    earlier = dot(before.astype(bf16), named.astype(bf16)).astype(i32)
    return named > 0, earlier, wanted


def request_body(
    capacity,
    core_ref,
    owner_hbm,
    local_hbm,
    weight_hbm,
    labels_hbm,
    pairs_hbm,
    table_ref,
    codes_ref,
    weights_ref,
    label_ref,
    pairs_ref,
    owner_ref,
    local_ref,
    weight_ref,
    labels_ref,
    arrivals,
):
    del core_ref
    pairs = pltpu.make_async_copy(pairs_hbm, pairs_ref, arrivals.at[4])
    pairs.start()
    small = zip((owner_hbm, local_hbm, weight_hbm, labels_hbm), (owner_ref, local_ref, weight_ref, labels_ref))
    copies = [pltpu.make_async_copy(source, target, arrivals.at[i]) for i, (source, target) in enumerate(small)]
    for copy in copies:
        copy.start()
    for copy in copies:
        copy.wait()
    groups = table_ref.shape[0]
    owner = owner_ref[...]
    seeds, neighbours = owner.shape
    named, earlier, wanted = places(capacity, groups, owner, local_ref[...])
    place = jnp.where(named, earlier, -1)
    slot = iota((capacity, groups), 0)
    table = jnp.zeros((capacity, groups), i32)
    for s in range(seeds):
        table = jnp.where(place[s : s + 1, :] == slot, wanted[s : s + 1, :], table)
    spare = jnp.zeros((LANES - capacity, groups), i32)
    table_ref[...] = jnp.concatenate([table, spare], axis=0).T
    code_of = coded_slots(iota((seeds, groups), 1) * capacity + earlier)
    owner_t = owner.T
    weight_t = weight_ref[...].T
    lane = iota((neighbours, groups), 1)
    own = []
    for s in range(seeds):
        own.append(jnp.where(owner_t[:, s : s + 1] == lane, code_of[s : s + 1, :], 0.0).astype(bf16))
        rows = pl.ds(s * neighbours, neighbours)
        weights_ref[rows, :] = jnp.broadcast_to(weight_t[:, s : s + 1], (neighbours, weights_ref.shape[1]))
    everything = jnp.ones((groups, codes_ref.shape[1]), bf16)
    codes_ref[...] = dot(jnp.concatenate(own, axis=0), everything).astype(bf16)
    diagonal = iota((seeds, seeds), 0) == iota((seeds, seeds), 1)
    label = jnp.sum(jnp.where(diagonal, labels_ref[...].astype(f32), 0.0), axis=1, keepdims=True)
    label_ref[...] = label.astype(i32)
    pairs.wait()


def coded_slots(slot):
    return ((128 + (slot & 127)) * (1 << (slot >> 7))).astype(f32)


def serve_body(
    capacity,
    asked_ref,
    pairs_ref,
    first_hbm,
    second_hbm,
    third_t_hbm,
    rows_ref,
    first_ref,
    second_ref,
    third_t_ref,
    stage_ref,
    wide_ref,
    turned_ref,
    index_ref,
    arrival,
    params,
):
    layers = zip((first_hbm, second_hbm, third_t_hbm), (first_ref, second_ref, third_t_ref))
    copies = [pltpu.make_async_copy(source, target, params.at[i]) for i, (source, target) in enumerate(layers)]
    asked = asked_ref[...]
    turned_ref[...] = asked.T[:capacity, :] >> 1
    index = pltpu.make_async_copy(turned_ref, index_ref, arrival)
    index.start()
    for copy in copies:
        copy.start()
    index.wait()
    odd = (asked & 1) > 0
    groups = wide_ref.shape[0]
    size = asked.shape[0] // groups
    for group in range(groups):
        span = slice(group * size, (group + 1) * size)
        for p in range(capacity):
            stage = stage_ref.at[p % stage_ref.shape[0]]
            for source in range(size):
                stage[2 * source : 2 * source + 2, :] = pairs_ref[index_ref[p, span.start + source]].astype(f32)
            first = stage[pl.ds(0, size, stride=2), :]
            second = stage[pl.ds(1, size, stride=2), :]
            wide_ref[group, pl.ds(p, size, stride=capacity), :] = jnp.where(odd[span, p : p + 1], second, first)
        rows_ref[span] = wide_ref[group, : size * capacity, :].reshape(size, capacity, -1).astype(bf16)
    for copy in copies:
        copy.wait()


def step_body(
    total_seeds,
    blocks,
    core_ref,
    codes_ref,
    arrived_ref,
    weights_ref,
    label_ref,
    first_ref,
    second_ref,
    third_t_ref,
    logits_hbm,
    send_ref,
    terms_ref,
    x_ref,
    first_act_ref,
    weighted_ref,
    second_act_ref,
    second_grad_ref,
    first_grad_ref,
    grads_ref,
    logits_ref,
    leaving,
):
    seeds, classes = logits_ref.shape
    rows = codes_ref.shape[0]
    neighbours = rows // seeds
    zero = jnp.zeros((), bf16)
    own_rows = [slice(b * rows // blocks, (b + 1) * rows // blocks) for b in range(blocks)]
    own_seeds = [slice(b * seeds // blocks, (b + 1) * seeds // blocks) for b in range(blocks)]
    size, seed_size = rows // blocks, seeds // blocks

    def rectified(pre):
        return jnp.maximum(pre.astype(bf16), zero)

    def masked(act, grad):
        return jnp.where(act > zero, grad.astype(bf16), zero)

    def halves(ref, parts):
        wide = ref.shape[2]
        for part, r in zip(parts, own_rows):
            for h in range(2):
                ref[h, r, :] = part[:, h * wide : (h + 1) * wide]

    slots = arrived_ref.shape[0]
    side = slots // 2
    arrived = jnp.concatenate([arrived_ref[:side, :], arrived_ref[side:, :]], axis=1)
    every_code = coded_slots(iota((16, side), 1)).astype(bf16)
    every_code = jnp.concatenate([every_code] * (size // 16), axis=0)
    bound = float(128 << (side >> 7))
    x = []
    for r in own_rows:
        late = codes_ref[r, :] >= jnp.asarray(bound, bf16)
        code = jnp.where(late, codes_ref[r, :] * jnp.asarray(128.0 / bound, bf16), codes_ref[r, :])
        code = jnp.concatenate([code] * (side // LANES), axis=1)
        pick = jnp.where(code == every_code, jnp.ones((), bf16), zero)
        both = dot(pick, arrived).astype(bf16)
        x.append(jnp.where(late, both[:, LANES:], both[:, :LANES]))
        x_ref[r, :] = x[-1]
    first_act = [rectified(dot(part, first_ref[...])) for part in x]
    second_act = [rectified(dot(part, second_ref[...])) for part in first_act]
    for part, r in zip(first_act, own_rows):
        first_act_ref[r, :] = part
    halves(second_act_ref, second_act)
    weighted, terms = [], []
    for act, r, s in zip(second_act, own_rows, own_seeds):
        row_logits = dot(act, third_t_ref[...], ((1,), (1,)))
        weight = weights_ref[r, :]
        weight = jnp.concatenate([weight, weight[:, : classes - LANES]], axis=1)
        logits = jnp.sum((weight * row_logits).reshape(seed_size, neighbours, classes), axis=1)
        logits_ref[s, :] = logits
        highest = jnp.max(logits, axis=1, keepdims=True)
        log_total = jnp.log(jnp.sum(jnp.exp(logits - highest), axis=1, keepdims=True)) + highest
        onehot = jnp.where(label_ref[s, :] == iota((seed_size, classes), 1), 1.0, 0.0)
        terms.append(log_total - jnp.sum(onehot * logits, axis=1, keepdims=True))
        logit_grad = (jnp.exp(logits - log_total) - onehot) / total_seeds
        every = jnp.broadcast_to(logit_grad[:, None, :], (seed_size, neighbours, classes)).reshape(size, classes)
        weighted.append((weight * every).astype(bf16))
        weighted_ref[r, :] = weighted[-1]
    logits_copy = pltpu.make_async_copy(logits_ref, logits_hbm, leaving)
    logits_copy.start()
    second_grad = [masked(a, dot(g, third_t_ref[...])) for a, g in zip(second_act, weighted)]
    halves(second_grad_ref, second_grad)
    first_grad = [masked(a, dot(g, second_ref[...], ((1,), (1,)))) for a, g in zip(first_act, second_grad)]
    halves(first_grad_ref, first_grad)
    diagonal = iota((seeds, LANES), 0) == iota((seeds, LANES), 1)
    loss_row = jnp.sum(jnp.where(diagonal, jnp.concatenate(terms, axis=0), 0.0), axis=0, keepdims=True)
    loss_row = loss_row.astype(bf16).astype(f32)
    terms_ref[...] = jnp.broadcast_to(loss_row, terms_ref.shape)
    other = 1 - core_ref[0]
    write_half(
        grads_ref, loss_row, x_ref, first_act_ref, weighted_ref, second_act_ref, second_grad_ref, first_grad_ref, other
    )
    send_ref[...] = grads_ref[...].astype(bf16)
    logits_copy.wait()


def write_half(out_ref, loss_row, x_ref, first_act_ref, weighted_ref, second_act_ref, second_grad_ref, first_grad_ref, half):
    down = ((0,), (0,))
    first = dot(x_ref[...], first_grad_ref[half], down)
    second = dot(first_act_ref[...], second_grad_ref[half], down)
    third = dot(weighted_ref[...], second_act_ref[half], down)
    parts = first.shape[1] // LANES
    tall = out_ref.shape[0] // parts
    for j in range(parts):
        at = j * tall
        for piece in (first, second, third):
            out_ref[at : at + piece.shape[0], :] = piece[:, j * LANES : (j + 1) * LANES]
            at += piece.shape[0]
        out_ref[at : (j + 1) * tall, :] = jnp.zeros(((j + 1) * tall - at, LANES), f32)
        out_ref[at : at + 1, :] = loss_row


def keep_body(
    core_ref, terms_ref, x_ref, first_act_ref, weighted_ref, second_act_ref, second_grad_ref, first_grad_ref, keep_ref
):
    write_half(
        keep_ref,
        terms_ref[:1, :],
        x_ref,
        first_act_ref,
        weighted_ref,
        second_act_ref,
        second_grad_ref,
        first_grad_ref,
        core_ref[0],
    )


def total_body(chips, parts_ref, total_ref):
    rows = parts_ref.shape[0]
    chunk = rows // chips
    tall = -(-chunk // 8) * 8
    column = iota((tall, rows), 1)
    which = ((column.astype(f32) + 0.5) / chunk).astype(i32)
    same = jnp.where(column - which * chunk == iota((tall, rows), 0), 1.0, 0.0).astype(bf16)
    total = dot(same, parts_ref[...]).astype(bf16)
    total_ref[...] = dot(same, total, ((0,), (0,))).astype(bf16)


def columns(half, half_ref, outs, stages, arrivals):
    copies = []
    at = 0
    for i, (out, stage) in enumerate(zip(outs, stages)):
        size, wide = stage.shape
        parts = wide // LANES
        tall = half_ref.shape[0] // parts
        for j in range(parts):
            stage[:, j * LANES : (j + 1) * LANES] = half_ref[j * tall + at : j * tall + at + size, :].astype(f32)
        span = pl.ds(pl.multiple_of(half * wide, wide), wide)
        copies.append(pltpu.make_async_copy(stage, out.at[:, span], arrivals.at[i]))
        copies[-1].start()
        at += size
    for copy in copies:
        copy.wait()


def own_body(total_seeds, core_ref, own_ref, first_hbm, second_hbm, third_t_hbm, loss_hbm, loss_ref, leaving, *scratch):
    outs = (first_hbm, second_hbm, third_t_hbm)
    at = sum(out.shape[0] for out in outs)
    loss_ref[...] = jnp.sum(own_ref[at : at + 1, :].astype(f32), axis=1, keepdims=True) / total_seeds
    copy = pltpu.make_async_copy(loss_ref, loss_hbm, leaving)
    copy.start()
    columns(core_ref[0], own_ref, outs, scratch[:3], scratch[3])
    copy.wait()


def other_body(core_ref, other_ref, given_first, given_second, given_third_t, first_hbm, second_hbm, third_t_hbm, *scratch):
    del given_first, given_second, given_third_t
    columns(1 - core_ref[0], other_ref, (first_hbm, second_hbm, third_t_hbm), scratch[:3], scratch[3])


def everywhere(parts, axis):
    return lax.all_to_all(parts, axis, 0, 0, tiled=True)


def on_device(features, nbr_owner, nbr_local, ppr_weight, labels, w_first, w_second, w_third):
    groups = lax.axis_size(NODES)
    chips = lax.axis_size(CHIPS)
    seeds, neighbours = nbr_owner.shape
    capacity = min(seeds, 2 * seeds * neighbours // groups)
    width, hidden = w_first.shape
    classes = w_third.shape[1]
    total_seeds = float(seeds * groups)
    slots = groups * capacity
    shape = jax.ShapeDtypeStruct
    core = lax.axis_index(CORE).astype(i32).reshape(1)
    swap = [(0, 1), (1, 0)]

    pairs = features.reshape(-1, 2, width)
    rows = seeds * neighbours
    table, codes, weights, label, pairs = call(
        functools.partial(request_body, capacity),
        (
            shape((groups, LANES), i32),
            shape((rows, LANES), bf16),
            shape((rows, LANES), f32),
            shape((seeds, 1), i32),
            pltpu.VMEM(pairs.shape, bf16),
        ),
        [SMEM] + [FAR] * 5,
        [
            *(pltpu.VMEM((seeds, neighbours), t) for t in (i32, i32, f32)),
            pltpu.VMEM((1, seeds), i32),
            pltpu.SemaphoreType.DMA((5,)),
        ],
    )(
        core,
        *(
            pltpu.with_memory_space_constraint(a, pltpu.HBM)
            for a in (nbr_owner, nbr_local, ppr_weight, labels.reshape(1, -1), pairs)
        ),
    )
    asked = everywhere(table.reshape(groups, 1, LANES), NODES).reshape(groups, LANES)
    params = (w_first, w_second, w_third.T)
    served, *params = call(
        functools.partial(serve_body, capacity),
        (shape((groups, capacity, width), bf16), *(pltpu.VMEM(p.shape, bf16) for p in params)),
        [VMEM, VMEM, FAR, FAR, FAR],
        [
            pltpu.VMEM((4, groups // 2 + 8, width), f32),
            pltpu.VMEM((4, (groups // 4 + 1) * capacity, width), f32),
            pltpu.VMEM((capacity, groups), i32),
            pltpu.SMEM((capacity, groups), i32),
            pltpu.SemaphoreType.DMA,
            pltpu.SemaphoreType.DMA((3,)),
        ],
        16,
    )(asked, pairs, *(pltpu.with_memory_space_constraint(p, pltpu.HBM) for p in params))
    arrived = everywhere(served, NODES).reshape(slots, width)

    half = hidden // 2
    blocks = half // LANES
    tall = 2 * chips // blocks * -(-(width + hidden + classes + 1) * blocks // (2 * chips))
    grads = (blocks * tall, LANES)
    seed_logits, send, *kept = call(
        functools.partial(step_body, total_seeds, 2),
        (
            pltpu.HBM((seeds, classes), f32),
            shape(grads, bf16),
            shape((8, LANES), f32),
            shape((rows, width), bf16),
            shape((rows, hidden), bf16),
            shape((rows, classes), bf16),
            *(shape((2, rows, half), bf16) for _ in range(3)),
        ),
        [SMEM] + [VMEM] * 7,
        [pltpu.VMEM(grads, f32), pltpu.VMEM((seeds, classes), f32), pltpu.SemaphoreType.DMA],
        32,
        (FAR, *[VMEM] * 8),
    )(core, codes, arrived, weights, label, *params)
    near = lax.ppermute(send, CORE, swap)
    keep = call(keep_body, shape(grads, f32), [SMEM] + [VMEM] * 7, (), 16)(core, *kept)
    parts = (keep + near.astype(f32)).astype(bf16)
    mine = everywhere(parts.reshape(-1, 2, LANES), CHIPS).reshape(grads)
    totals = call(functools.partial(total_body, chips), shape(grads, bf16), [VMEM])(mine)
    own = everywhere(totals.reshape(-1, 2, LANES), CHIPS).reshape(grads)
    other = lax.ppermute(own, CORE, swap)
    sizes = (width, hidden, classes)
    scratch = [*(pltpu.VMEM((n, half), f32) for n in sizes), pltpu.SemaphoreType.DMA((3,))]
    sums = tuple(pltpu.HBM((n, hidden), f32) for n in sizes)
    *started, loss = call(
        functools.partial(own_body, total_seeds),
        (*sums, pltpu.HBM((1, 1), f32)),
        [SMEM, VMEM],
        [pltpu.VMEM((1, 1), f32), pltpu.SemaphoreType.DMA, *scratch],
        8,
        FAR,
    )(core, own)
    grad_first, grad_second, grad_third_t = call(
        other_body, sums, [SMEM, VMEM, FAR, FAR, FAR], scratch, 8, FAR, {2: 0, 3: 1, 4: 2}
    )(core, other, *started)
    return (loss.reshape(()), seed_logits, grad_first, grad_second, grad_third_t.T)


def solution(mesh):
    finer = Mesh(mesh.devices.reshape(4, 4, 4, 2), NODES)
    placed = (
        P(NODES, None),
        P(NODES, None),
        P(NODES, None),
        P(NODES, None),
        P(NODES),
        P(),
        P(),
        P(),
    )
    return jax.shard_map(
        on_device,
        mesh=finer,
        in_specs=placed,
        out_specs=(P(), P(NODES, None), P(), P(), P()),
        check_vma=False,
    )
```
